256 devices in a mesh: pipe: 8 (over x, core), dp: 32 (over z, y).
Axes of the slice: x: 4, y: 4, z: 8, core: 2. Of those that a mesh axis runs over, the one named last changes fastest.
Arguments:
- x_ckpt: bfloat16 [8, 2, 32, 512, 512], P('pipe', None, 'dp'), may hold values from -6 to 6
- top_cot: bfloat16 [2, 32, 512, 512], P(None, 'dp'), may hold values from -6 to 6
- skip_cot: bfloat16 [2, 32, 512, 512], P(None, 'dp'), may hold values from -6 to 6
- w_conv: bfloat16 [8, 512, 3, 1024], P('pipe', 'dp'), may hold values from -0.15625 to 0.15625
- w_mix: bfloat16 [8, 512, 1024], P('pipe', 'dp'), may hold values from -0.25 to 0.25
Outputs:
- cot_inputs: bfloat16 [8, 2, 32, 512, 512], P('pipe', None, 'dp')
- grad_conv: float32 [8, 512, 3, 1024], P('pipe', 'dp')
- grad_mix: float32 [8, 512, 1024], P('pipe', 'dp')
The draws below stay inside these ranges and needn't reach their ends.
All inputs are finite; a program needn't handle non-finite values.
Results may differ from the reference program's by a relative error of at most 0.014.
Values may be sent and summed in bfloat16 or wider, within the bound.
A program may use at most 128 MiB of HBM per device.

```python
import jax
import jax.numpy as jnp
from jax import lax

C = 512
MB = 2
LEN = 512
BATCH = 32
N_PIPE = 8


def with_spikes(drawn, key, source, target, shards_of, factor):
    owner, partner = [(jnp.arange(drawn.shape[dim]) // (drawn.shape[dim] // shards_of)).reshape([-1 if axis == dim else 1 for axis in range(drawn.ndim)]) for dim in (source, target)]
    chosen = jax.random.permutation(key, shards_of)[partner]
    strong = (owner == chosen) | (owner == (partner + shards_of // 2) % shards_of)
    return jnp.where(strong, factor * drawn, drawn)


def levels(stream_key, dims, pieces, least, top_value):
    loudness, own = 1.0, jax.random.fold_in(stream_key, 6)
    for axis_at, parts in pieces:
        steps = jnp.exp(jax.random.uniform(jax.random.fold_in(own, axis_at), (parts,), jnp.float32, least / len(pieces), top_value / len(pieces)))
        loudness = loudness * jnp.repeat(steps, dims[axis_at] // parts).reshape([-1 if axis == axis_at else 1 for axis in range(len(dims))])
    return loudness


def scatter_about(stream_key, extent, deviation, bound, cuts=(), kind=jnp.bfloat16):
    drawn = jax.random.normal(stream_key, extent, jnp.float32) * deviation
    if len(cuts) > 0:
        drawn = levels(stream_key, extent, cuts, -0.22, 0.18) * drawn
    return jnp.clip(drawn, min=-bound, max=bound).astype(kind)


def noise_with(key, extent, deviation, most, split, heavy, kind=jnp.bfloat16):
    array = deviation * jax.random.normal(key, extent, jnp.float32)
    if split:
        array = array * levels(key, extent, split, -0.22, 0.18)
    return jnp.clip(with_spikes(array, jax.random.fold_in(key, 3), *heavy), -most, most).astype(kind)


def setup_inputs(seed: int = 0) -> dict:
    key_of = jax.random.split(jax.random.key(seed), 6)
    x_ckpt = noise_with(key_of[0], (N_PIPE, MB, BATCH, LEN, C), 1.0, 6.0, ((0, 8), (2, 32)), (2, 4, 32, 2.75))
    top_cot = scatter_about(key_of[1], (MB, BATCH, LEN, C), 1.0, 6.0, ((1, 32),))
    skip_cot = scatter_about(key_of[2], (MB, BATCH, LEN, C), 1.0, 6.0, ((1, 32),))
    w_conv = scatter_about(key_of[3], (N_PIPE, C, 3, 2 * C), (3 * C) ** -0.5, 0.15625, ((0, 8), (1, 32)))
    w_mix = scatter_about(key_of[4], (N_PIPE, C, 2 * C), C ** -0.5, 0.25, ((0, 8), (1, 32)))
    return dict(x_ckpt=x_ckpt, top_cot=top_cot, skip_cot=skip_cot, w_conv=w_conv, w_mix=w_mix)


def delay_seq(signal, shift_by):
    samples = signal.shape[1]
    rolled = jnp.roll(signal, shift_by, axis=1)
    positions = lax.broadcasted_iota(jnp.int32, (1, samples, 1), 1)
    return jnp.where(positions >= shift_by, rolled, jnp.zeros_like(rolled))


def advance_seq(signal, shift_by):
    samples = signal.shape[1]
    rolled = jnp.roll(signal, -shift_by, axis=1)
    positions = lax.broadcasted_iota(jnp.int32, (1, samples, 1), 1)
    return jnp.where(positions < samples - shift_by, rolled, jnp.zeros_like(rolled))


def layer_back(x_rows, grad_next, skip_grad, conv_w, mix_w, dilation):
    channels = x_rows.shape[2]
    tapped_x = jnp.stack([delay_seq(x_rows, offset * dilation) for offset in range(3)], axis=2)
    pre_act = jnp.einsum("slkc,ckn->sln", tapped_x.astype(jnp.float32), conv_w.astype(jnp.float32))
    filter_act = jnp.tanh(pre_act[..., :channels])
    gate_act = jax.nn.sigmoid(pre_act[..., channels:])
    hidden = (filter_act * gate_act).astype(jnp.bfloat16)
    cot_pair = jnp.concatenate([grad_next, skip_grad], axis=2)
    hid_grad = jnp.einsum("sln,cn->slc", cot_pair.astype(jnp.float32), mix_w.astype(jnp.float32))
    pre_grad = jnp.concatenate([hid_grad * gate_act * (1.0 - filter_act * filter_act),
                                hid_grad * filter_act * gate_act * (1.0 - gate_act)], axis=2).astype(jnp.bfloat16)
    back_taps = jnp.einsum("sln,ckn->slkc", pre_grad.astype(jnp.float32), conv_w.astype(jnp.float32))
    input_grad = grad_next.astype(jnp.float32)
    for offset in range(3):
        input_grad = input_grad + advance_seq(back_taps[:, :, offset], offset * dilation)
    return input_grad.astype(jnp.bfloat16), tapped_x, hidden, pre_grad, cot_pair


def reference(x_ckpt, top_cot, skip_cot, w_conv, w_mix):
    rows_all = MB * BATCH
    skip_rows = skip_cot.reshape(rows_all, LEN, C)
    cot_next = top_cot.reshape(rows_all, LEN, C)
    cot_list = [None] * N_PIPE
    conv_list = [None] * N_PIPE
    mix_list = [None] * N_PIPE
    for sec_index in reversed(range(N_PIPE)):
        x_rows = x_ckpt[sec_index].reshape(rows_all, LEN, C)
        input_grad, tapped_x, hidden, pre_grad, cot_pair = layer_back(
            x_rows, cot_next, skip_rows, w_conv[sec_index], w_mix[sec_index], 2 ** sec_index)
        conv_list[sec_index] = jnp.einsum("slkc,sln->ckn", tapped_x.astype(jnp.float32), pre_grad.astype(jnp.float32))
        mix_list[sec_index] = jnp.einsum("slc,sln->cn", hidden.astype(jnp.float32), cot_pair.astype(jnp.float32))
        cot_list[sec_index] = input_grad.reshape(MB, BATCH, LEN, C)
        cot_next = input_grad
    return jnp.stack(cot_list), jnp.stack(conv_list), jnp.stack(mix_list)
```

```python
import functools
import heapq

import jax
import jax.numpy as jnp
from jax import lax
from jax.experimental import pallas as pl
from jax.experimental.pallas import tpu as pltpu
from jax.sharding import PartitionSpec as P

NZ, NY = 8, 4
UNIT = 128


def halves(piece):
    start, count = piece
    first = (count // UNIT + 1) // 2 * UNIT
    return (start, first), (start + first, count - first)


def wrap(offset, count):
    return (offset + count // 2 - 1) % count - (count // 2 - 1)


def gather_plan(split, width, rows, rate, lag):
    sizes = {"z": NZ, "y": NY}
    free, events, sends, order = {}, [], [], []
    seq = 0

    def send(now, group, axis, way, offset, piece):
        nonlocal seq
        if piece[1] == 0:
            return
        key = (axis, way)
        begin = max(now, free.get(key, 0.0))
        free[key] = begin + rows * piece[1] * 2 / rate
        ident = len(sends)
        shift = dict(offset)
        shift[axis] = wrap(shift[axis] - way, sizes[axis])
        sends.append((axis, way, dict(offset), shift, piece))
        order.append(("send", ident))
        heapq.heappush(events, (free[key] + lag, ident, group))
        seq += 1

    axes = (("z", "y"), ("y", "z"))
    pieces = ((0, split), (split, width - split))
    here = {"z": 0, "y": 0}
    for group in (0, 1):
        for way in (1, -1):
            send(0.0, group, axes[group][0], way, here, pieces[group])
    for group in (0, 1):
        for way in (1, -1):
            send(0.0, group, axes[group][1], way, here, pieces[group])
    last = 0.0
    while events:
        now, ident, group = heapq.heappop(events)
        last = now
        axis, way, _, offset, piece = sends[ident]
        order.append(("wait", ident))
        reach = sizes[axis] // 2
        done = abs(offset[axis]) if offset[axis] != reach else reach
        if done < reach - 1:
            send(now, group, axis, way, offset, piece)
        elif done == reach - 1:
            send(now, group, axis, way, offset, halves(piece)[0 if way > 0 else 1])
        if axis == axes[group][0]:
            for side in (1, -1):
                send(now, group, axes[group][1], side, offset, piece)
    return sends, order, last


def scatter_plan(split, width, rows, rate, lag, cost):
    sizes = {"z": NZ, "y": NY}
    axes = (("z", "y"), ("y", "z"))
    pieces = ((0, split), (split, width - split))
    tasks = {}
    for group in (0, 1):
        one, two = axes[group]
        h1, h2 = sizes[one] // 2, sizes[two] // 2
        part1 = halves(pieces[group])
        others = [h2] + [s * j for j in range(h2 - 1, 0, -1) for s in (1, -1)] + [0]
        for rank, o2 in enumerate(others):
            for way in (1, -1):
                for j in range(h1, 0, -1):
                    piece = pieces[group] if j < h1 else part1[0 if way > 0 else 1]
                    needs = [(group, 1, way, j + 1, o2)] if j < h1 else []
                    tasks[(group, 1, way, j, o2)] = dict(
                        axis=one, way=way, block={one: way * j, two: o2}, piece=piece,
                        recvs=needs, locals=[], rank=(rank, -j))
            tasks[(group, 1, 0, 0, o2)] = dict(
                axis=None, way=0, block={one: 0, two: o2}, piece=pieces[group],
                recvs=[(group, 1, 1, 1, o2), (group, 1, -1, 1, o2)], locals=[], rank=(rank, 0))
        for way in (1, -1):
            for j in range(h2, 0, -1):
                piece = pieces[group] if j < h2 else part1[0 if way > 0 else 1]
                needs = [(group, 2, way, j + 1, 0)] if j < h2 else []
                at = way * j if j < h2 else h2
                tasks[(group, 2, way, j, 0)] = dict(
                    axis=two, way=way, block={one: 0, two: at}, piece=piece,
                    recvs=needs, locals=[(group, 1, 0, 0, at)], rank=(-1, -j))
        tasks[(group, 2, 0, 0, 0)] = dict(
            axis=None, way=0, block={one: 0, two: 0}, piece=pieces[group],
            recvs=[(group, 2, 1, 1, 0), (group, 2, -1, 1, 0)], locals=[(group, 1, 0, 0, 0)], rank=(-1, 0))
    arrive, finished, free, order, clock = {}, {}, {}, [], 0.0
    left = dict(tasks)
    while left:
        best = None
        for key, task in left.items():
            if any(n not in arrive for n in task["recvs"]) or any(n not in finished for n in task["locals"]):
                continue
            ready = max([clock] + [arrive[n] for n in task["recvs"]] + [finished[n] for n in task["locals"]])
            link = free.get((task["axis"], task["way"]), 0.0) if task["axis"] else 0.0
            score = (ready, task["rank"], link, key)
            if best is None or score < best[0]:
                best = (score, key, ready)
        _, key, ready = best
        task = left.pop(key)
        clock = ready + cost * rows * task["piece"][1]
        finished[key] = clock
        if task["axis"]:
            lane = (task["axis"], task["way"])
            begin = max(clock, free.get(lane, 0.0))
            free[lane] = begin + rows * task["piece"][1] * 2 / rate
            arrive[key] = free[lane] + lag
        order.append(key)
    return tasks, order, clock


F32, BF16 = jnp.float32, jnp.bfloat16
MESH = pl.DeviceIdType.MESH
SECTIONS = 8
C = 512
LEN = 512
ROWS = 1024
SHARD = 16
WIDTH = 4096
CONV = 3072
RES = slice(3072, 3584)
SKIP = slice(3584, 4096)
CHUNK = 256
CHUNKS = ROWS // CHUNK
PER_SEQ = LEN // CHUNK
PAD = 264
STRIDE = LEN + PAD
RATE, LAG = 46.5e3, 1.8
AG_SPLIT, RS_SPLIT = 2560, 1536
NT = (((1,), (1,)), ((), ()))


def dot(a, b):
    return jnp.dot(a, b, preferred_element_type=F32)


def dot_nt(a, b):
    return lax.dot_general(a, b, NT, preferred_element_type=F32)


def kernel(gather, scatter, slots, x_hbm, top_hbm, skip_hbm, w_hbm, cot_hbm, grad_hbm,
           w_v, x_v, xf_v, xt_v, ht_v, a1_v, a2_v, hs_v, pf_v, a_v, out_v, g_v,
           ra_v, rb_v, sa_v, sb_v,
           ag_send, ag_recv, rs_send, rs_recv, ch_send, ch_recv, ld_sem, st_sem):
    p = lax.axis_index("pipe")
    dp = lax.axis_index("dp")
    z, y = dp // NY, lax.rem(dp, NY)

    def dp_at(dz, dy):
        return lax.rem(z + (dz + NZ), NZ) * NY + lax.rem(y + (dy + NY), NY)

    def rows_at(offset):
        return pl.ds(pl.multiple_of(dp_at(offset["z"], offset["y"]) * SHARD, SHARD), SHARD)

    def peer(axis, way):
        return {"dp": dp_at(way, 0) if axis == "z" else dp_at(0, way)}

    is_last, is_first = p == SECTIONS - 1, p == 0

    x_load = pltpu.make_async_copy(x_hbm, x_v, ld_sem.at[0])
    skip_load = pltpu.make_async_copy(skip_hbm, a_v.at[:, SKIP], ld_sem.at[1])
    top_load = pltpu.make_async_copy(top_hbm, a_v.at[:, RES], ld_sem.at[2])
    own_load = pltpu.make_async_copy(w_hbm, w_v.at[rows_at({"z": 0, "y": 0}), :], ld_sem.at[3])
    x_load.start()
    skip_load.start()
    own_load.start()

    @pl.when(is_last)
    def _():
        top_load.start()

    barrier = pltpu.get_barrier_semaphore()
    for axis in ("z", "y"):
        for way in (1, -1):
            pl.semaphore_signal(barrier, inc=1, device_id=peer(axis, way), device_id_type=MESH)

    for way in (1, SECTIONS - 1):
        neighbour = {"pipe": lax.rem(p + way, SECTIONS)}
        pl.semaphore_signal(barrier, inc=1, device_id=neighbour, device_id_type=MESH)
    pl.semaphore_wait(barrier, 6)

    ag_sends, ag_order, _ = gather

    def ag_send_copy(ident):
        axis, way, offset, _, piece = ag_sends[ident]
        lanes = slice(piece[0], piece[0] + piece[1])
        here = w_v.at[rows_at(offset), lanes]
        own = offset["z"] == 0 and offset["y"] == 0
        source = w_hbm.at[:, lanes] if own else here
        return pltpu.make_async_remote_copy(
            source, here, ag_send.at[ident], ag_recv.at[ident],
            device_id=peer(axis, way), device_id_type=MESH)

    def ag_recv_copy(ident):
        axis, way, _, landed, piece = ag_sends[ident]
        lanes = slice(piece[0], piece[0] + piece[1])
        there = w_v.at[rows_at(landed), lanes]
        return pltpu.make_async_remote_copy(
            there, there, ag_send.at[ident], ag_recv.at[ident],
            device_id=peer(axis, -way), device_id_type=MESH)

    started = False
    for what, ident in ag_order:
        if what == "send":
            ag_send_copy(ident).start()
            continue
        if not started:
            started = True
            x_load.wait()
            for s in range(2):
                xf_v[s * STRIDE:s * STRIDE + PAD, :] = jnp.zeros((PAD, C), F32)
                xf_v[s * STRIDE + PAD:(s + 1) * STRIDE, :] = x_v[s * LEN:(s + 1) * LEN, :].astype(F32)
                pf_v[s * STRIDE + LEN:(s + 1) * STRIDE, :] = jnp.zeros((PAD, 2 * C), F32)
        ag_recv_copy(ident).wait_recv()
    own_load.wait()
    skip_load.wait()

    d = (1 + lax.rem(p, 2)) * (1 + 3 * lax.rem(p // 2, 2)) * (1 + 15 * (p // 4))

    def shifted(ref, base, shift_down, shift):
        window = ref[pl.ds(pl.multiple_of(base, 8), CHUNK + 8), :]
        return pltpu.roll(window, shift_down, 0)[8:8 + CHUNK].astype(BF16)

    def delayed(s, t, shift):
        down = lax.rem(shift, 8)
        return shifted(xf_v, s * STRIDE + PAD + t - (shift - down) - 8, down, shift)

    def advanced(s, t, shift):
        down = lax.rem(8 - lax.rem(shift, 8), 8)
        return shifted(pf_v, s * STRIDE + t + (shift + down) - 8, down, shift)

    def place(q):
        s = q // PER_SEQ
        t = (PER_SEQ - 1 - lax.rem(q, PER_SEQ)) * CHUNK
        row = pl.multiple_of(s * LEN + t, CHUNK)
        return s, t, pl.ds(row, CHUNK)

    def forward(q):
        s, t, rows = place(q)
        x0 = x_v[rows, :]
        pre = dot(x0, w_v[:, 0:1024])
        pre = pre + dot(delayed(s, t, d), w_v[:, 1024:2048])
        pre = pre + dot(delayed(s, t, 2 * d), w_v[:, 2048:3072])
        filt = jnp.tanh(pre[:, :C])
        gate = jax.nn.sigmoid(pre[:, C:])
        a1_v[rows, :] = gate * (1.0 - filt * filt)
        hid = filt * gate
        a2_v[rows, :] = hid * (1.0 - gate)
        ht_v[:, rows] = hid.astype(BF16).T
        xt_v[:, rows] = x0.T
        hs_v[rows, :] = dot_nt(a_v[rows, SKIP], w_v[:, SKIP])

    def forward_step(q, carry):
        forward(q)
        return carry

    lax.fori_loop(0, jnp.where(is_last, 1, CHUNKS), forward_step, 0)

    @pl.when(is_last)
    def _():
        top_load.wait()

    def chain_send(q):
        _, _, rows = place(q)
        return pltpu.make_async_remote_copy(
            out_v.at[rows, :], a_v.at[rows, RES], ch_send.at[q], ch_recv.at[q],
            device_id={"pipe": p - 1}, device_id_type=MESH)

    def chain_recv(q):
        _, _, rows = place(q)
        return pltpu.make_async_remote_copy(
            a_v.at[rows, RES], a_v.at[rows, RES], ch_send.at[q], ch_recv.at[q],
            device_id={"pipe": p + 1}, device_id_type=MESH)

    def chain_store(q):
        _, _, rows = place(q)
        return pltpu.make_async_copy(out_v.at[rows, :], cot_hbm.at[rows, :], st_sem.at[q])

    def chain_step(q, carry):
        s, t, rows = place(q)

        @pl.when(jnp.logical_not(is_last))
        def _():
            chain_recv(q).wait_recv()

        g = a_v[rows, RES]
        hg = hs_v[rows, :] + dot_nt(g, w_v[:, RES])
        pg1 = (hg * a1_v[rows, :]).astype(BF16)
        pg2 = (hg * a2_v[rows, :]).astype(BF16)
        a_v[rows, 0:C] = pg1
        a_v[rows, C:2 * C] = pg2
        prow = pl.ds(pl.multiple_of(s * STRIDE + t, 8), CHUNK)
        pf_v[prow, 0:C] = pg1.astype(F32)
        pf_v[prow, C:2 * C] = pg2.astype(F32)
        a_v[rows, 1024:2048] = advanced(s, t, d)
        a_v[rows, 2048:3072] = advanced(s, t, 2 * d)
        out = g.astype(F32) + dot_nt(a_v[rows, 0:CONV], w_v[:, 0:CONV])
        out_v[rows, :] = out.astype(BF16)

        @pl.when(jnp.logical_not(is_first))
        def _():
            chain_send(q).start()

        chain_store(q).start()

        @pl.when(jnp.logical_and(is_last, q < CHUNKS - 1))
        def _():
            forward(jnp.minimum(q + 1, CHUNKS - 1))

        return carry

    lax.fori_loop(0, CHUNKS, chain_step, 0)

    def grad_step(lhs_v, n, carry):
        lanes = pl.ds(pl.multiple_of(n * C, C), C)
        g_v[:, lanes] = dot(lhs_v[...], a_v[:, lanes])
        return carry

    lax.fori_loop(0, 6, functools.partial(grad_step, xt_v), 0)
    lax.fori_loop(6, 8, functools.partial(grad_step, ht_v), 0)

    rs_tasks, rs_order, _ = scatter
    starts = (0, RS_SPLIT)
    recv_bufs, send_bufs = (ra_v, rb_v), (sa_v, sb_v)

    def rs_copy(key):
        task = rs_tasks[key]
        group, slot, sem = slots[key]
        lo = task["piece"][0] - starts[group]
        lanes = slice(lo, lo + task["piece"][1])
        source = send_bufs[group].at[slot, :, lanes]
        target = recv_bufs[group].at[slot, :, lanes]
        return pltpu.make_async_remote_copy(
            source, target, rs_send.at[sem], rs_recv.at[sem],
            device_id=peer(task["axis"], task["way"]), device_id_type=MESH)

    def rs_take(key):
        task = rs_tasks[key]
        group, slot, sem = slots[key]
        lo = task["piece"][0] - starts[group]
        view = recv_bufs[group].at[slot, :, lo:lo + task["piece"][1]]
        pltpu.make_async_remote_copy(
            view, view, rs_send.at[sem], rs_recv.at[sem],
            device_id=peer(task["axis"], -task["way"]), device_id_type=MESH).wait_recv()
        return group, slot, task["piece"]

    for key in rs_order:
        task = rs_tasks[key]
        rows = rows_at({"z": task["block"]["z"], "y": task["block"]["y"]})
        first, count = task["piece"]
        got = [rs_take(need) for need in task["recvs"]]
        if task["axis"] is None:
            total = g_v[rows, first:first + count]
            for group, slot, piece in got:
                total = total + recv_bufs[group][slot, :, 0:count].astype(F32)
            g_v[rows, first:first + count] = total
            continue
        group, slot, _ = slots[key]
        base = starts[group]
        spans = [(first, count, None)]
        if got:
            _, have, (p0, pn) = got[0]
            spans = [(p0, pn, have)]
            if p0 > first:
                spans.append((first, p0 - first, None))
            if p0 + pn < first + count:
                spans.append((p0 + pn, first + count - p0 - pn, None))
        for lo, n, have in spans:
            value = g_v[rows, lo:lo + n]
            if have is not None:
                value = value + recv_bufs[group][have, :, lo - base:lo - base + n].astype(F32)
            send_bufs[group][slot, :, lo - base:lo - base + n] = value.astype(BF16)
        rs_copy(key).start()

    grad_store = pltpu.make_async_copy(g_v.at[rows_at({"z": 0, "y": 0}), :], grad_hbm, ld_sem.at[0])
    grad_store.start()

    for ident in range(len(ag_sends)):
        ag_send_copy(ident).wait_send()
    for key in rs_order:
        if rs_tasks[key]["axis"] is not None:
            rs_copy(key).wait_send()
    for q in range(CHUNKS):
        chain_store(q).wait()

        @pl.when(jnp.logical_not(is_first))
        def _():
            chain_send(q).wait_send()

    grad_store.wait()


def local(x_ckpt, top_cot, skip_cot, w_conv, w_mix):
    x = x_ckpt.reshape(ROWS, C)
    top = top_cot.reshape(ROWS, C)
    skip = skip_cot.reshape(ROWS, C)
    w = jnp.concatenate([w_conv.reshape(SHARD, CONV), w_mix.reshape(SHARD, 2 * C)], axis=1)
    gather = gather_plan(AG_SPLIT, WIDTH, SHARD, RATE, LAG)
    scatter = scatter_plan(RS_SPLIT, WIDTH, SHARD, RATE, LAG, 2e-6)
    slots, counts, sems = {}, [0, 0], 0
    for key, task in scatter[0].items():
        if task["axis"] is not None:
            slots[key] = (key[0], counts[key[0]], sems)
            counts[key[0]] += 1
            sems += 1
    sends = len(gather[0])
    anywhere = pl.BlockSpec(memory_space=pl.ANY)
    dma = pltpu.SemaphoreType.DMA
    cot, grad = pl.pallas_call(
        functools.partial(kernel, gather, scatter, slots),
        out_shape=(
            jax.ShapeDtypeStruct((ROWS, C), BF16),
            jax.ShapeDtypeStruct((SHARD, WIDTH), F32),
        ),
        in_specs=[anywhere] * 4,
        out_specs=(anywhere, anywhere),
        scratch_shapes=[
            pltpu.VMEM((C, WIDTH), BF16),
            pltpu.VMEM((ROWS, C), BF16),
            pltpu.VMEM((2 * STRIDE, C), F32),
            pltpu.VMEM((C, ROWS), BF16),
            pltpu.VMEM((C, ROWS), BF16),
            pltpu.VMEM((ROWS, C), F32),
            pltpu.VMEM((ROWS, C), F32),
            pltpu.VMEM((ROWS, C), F32),
            pltpu.VMEM((2 * STRIDE, 2 * C), F32),
            pltpu.VMEM((ROWS, WIDTH), BF16),
            pltpu.VMEM((ROWS, C), BF16),
            pltpu.VMEM((C, WIDTH), F32),
            pltpu.VMEM((counts[0], SHARD, RS_SPLIT), BF16),
            pltpu.VMEM((counts[1], SHARD, WIDTH - RS_SPLIT), BF16),
            pltpu.VMEM((counts[0], SHARD, RS_SPLIT), BF16),
            pltpu.VMEM((counts[1], SHARD, WIDTH - RS_SPLIT), BF16),
            dma((sends,)), dma((sends,)), dma((sems,)), dma((sems,)),
            dma((CHUNKS,)), dma((CHUNKS,)), dma((4,)), dma((CHUNKS,)),
        ],
        compiler_params=pltpu.CompilerParams(
            collective_id=0, has_side_effects=True, vmem_limit_bytes=67043328),
    )(x, top, skip, w)
    return (
        cot.reshape(x_ckpt.shape),
        grad[:, :CONV].reshape(w_conv.shape),
        grad[:, CONV:].reshape(w_mix.shape),
    )


def solution(mesh):
    placed = (
        P("pipe", None, "dp", None, None),
        P(None, "dp", None, None),
        P(None, "dp", None, None),
        P("pipe", "dp", None, None),
        P("pipe", "dp", None),
    )
    return jax.shard_map(
        local,
        mesh=mesh,
        in_specs=placed,
        out_specs=(
            P("pipe", None, "dp", None, None),
            P("pipe", "dp", None, None),
            P("pipe", "dp", None),
        ),
        check_vma=False,
    )
```

```python
import functools
import heapq

import jax
import jax.numpy as jnp
from jax import lax
from jax.experimental import pallas as pl
from jax.experimental.pallas import tpu as pltpu
from jax.sharding import PartitionSpec as P

NZ, NY = 8, 4
UNIT = 128


def halves(piece):
    start, count = piece
    first = (count // UNIT + 1) // 2 * UNIT
    return (start, first), (start + first, count - first)


def wrap(offset, count):
    return (offset + count // 2 - 1) % count - (count // 2 - 1)


def gather_plan(split, width, rows, rate, lag):
    sizes = {"z": NZ, "y": NY}
    free, events, sends, order = {}, [], [], []
    seq = 0

    def send(now, group, axis, way, offset, piece):
        nonlocal seq
        if piece[1] == 0:
            return
        key = (axis, way)
        begin = max(now, free.get(key, 0.0))
        free[key] = begin + rows * piece[1] * 2 / rate
        ident = len(sends)
        shift = dict(offset)
        shift[axis] = wrap(shift[axis] - way, sizes[axis])
        sends.append((axis, way, dict(offset), shift, piece))
        order.append(("send", ident))
        heapq.heappush(events, (free[key] + lag, ident, group))
        seq += 1

    axes = (("z", "y"), ("y", "z"))
    pieces = ((0, split), (split, width - split))
    here = {"z": 0, "y": 0}
    for group in (0, 1):
        for way in (1, -1):
            send(0.0, group, axes[group][0], way, here, pieces[group])
    for group in (0, 1):
        for way in (1, -1):
            send(0.0, group, axes[group][1], way, here, pieces[group])
    last = 0.0
    while events:
        now, ident, group = heapq.heappop(events)
        last = now
        axis, way, _, offset, piece = sends[ident]
        order.append(("wait", ident))
        reach = sizes[axis] // 2
        done = abs(offset[axis]) if offset[axis] != reach else reach
        if done < reach - 1:
            send(now, group, axis, way, offset, piece)
        elif done == reach - 1:
            send(now, group, axis, way, offset, halves(piece)[0 if way > 0 else 1])
        if axis == axes[group][0]:
            for side in (1, -1):
                send(now, group, axes[group][1], side, offset, piece)
    return sends, order, last


def scatter_plan(split, width, rows, rate, lag, cost):
    sizes = {"z": NZ, "y": NY}
    axes = (("z", "y"), ("y", "z"))
    pieces = ((0, split), (split, width - split))
    tasks = {}
    for group in (0, 1):
        one, two = axes[group]
        h1, h2 = sizes[one] // 2, sizes[two] // 2
        part1 = halves(pieces[group])
        others = [h2] + [s * j for j in range(h2 - 1, 0, -1) for s in (1, -1)] + [0]
        for rank, o2 in enumerate(others):
            for way in (1, -1):
                for j in range(h1, 0, -1):
                    piece = pieces[group] if j < h1 else part1[0 if way > 0 else 1]
                    needs = [(group, 1, way, j + 1, o2)] if j < h1 else []
                    tasks[(group, 1, way, j, o2)] = dict(
                        axis=one, way=way, block={one: way * j, two: o2}, piece=piece,
                        recvs=needs, locals=[], rank=(rank, -j))
            tasks[(group, 1, 0, 0, o2)] = dict(
                axis=None, way=0, block={one: 0, two: o2}, piece=pieces[group],
                recvs=[(group, 1, 1, 1, o2), (group, 1, -1, 1, o2)], locals=[], rank=(rank, 0))
        for way in (1, -1):
            for j in range(h2, 0, -1):
                piece = pieces[group] if j < h2 else part1[0 if way > 0 else 1]
                needs = [(group, 2, way, j + 1, 0)] if j < h2 else []
                at = way * j if j < h2 else h2
                tasks[(group, 2, way, j, 0)] = dict(
                    axis=two, way=way, block={one: 0, two: at}, piece=piece,
                    recvs=needs, locals=[(group, 1, 0, 0, at)], rank=(-1, -j))
        tasks[(group, 2, 0, 0, 0)] = dict(
            axis=None, way=0, block={one: 0, two: 0}, piece=pieces[group],
            recvs=[(group, 2, 1, 1, 0), (group, 2, -1, 1, 0)], locals=[(group, 1, 0, 0, 0)], rank=(-1, 0))
    arrive, finished, free, order, clock = {}, {}, {}, [], 0.0
    left = dict(tasks)
    while left:
        best = None
        for key, task in left.items():
            if any(n not in arrive for n in task["recvs"]) or any(n not in finished for n in task["locals"]):
                continue
            ready = max([clock] + [arrive[n] for n in task["recvs"]] + [finished[n] for n in task["locals"]])
            link = free.get((task["axis"], task["way"]), 0.0) if task["axis"] else 0.0
            score = (ready, task["rank"], link, key)
            if best is None or score < best[0]:
                best = (score, key, ready)
        _, key, ready = best
        task = left.pop(key)
        clock = ready + cost * rows * task["piece"][1]
        finished[key] = clock
        if task["axis"]:
            lane = (task["axis"], task["way"])
            begin = max(clock, free.get(lane, 0.0))
            free[lane] = begin + rows * task["piece"][1] * 2 / rate
            arrive[key] = free[lane] + lag
        order.append(key)
    return tasks, order, clock


F32, BF16 = jnp.float32, jnp.bfloat16
MESH = pl.DeviceIdType.MESH
SECTIONS = 8
C = 512
LEN = 512
ROWS = 1024
SHARD = 16
WIDTH = 4096
CONV = 3072
RES = slice(3072, 3584)
SKIP = slice(3584, 4096)
CHUNK = 256
CHUNKS = ROWS // CHUNK
PER_SEQ = LEN // CHUNK
PAD = 264
STRIDE = LEN + PAD
RATE, LAG = 46.5e3, 1.8
AG_SPLIT, RS_SPLIT = 2560, 1536
NT = (((1,), (1,)), ((), ()))


def dot(a, b):
    return jnp.dot(a, b, preferred_element_type=F32)


def dot_nt(a, b):
    return lax.dot_general(a, b, NT, preferred_element_type=F32)


def kernel(gather, scatter, slots, x_hbm, top_hbm, skip_hbm, wc_hbm, wm_hbm, cot_hbm, conv_hbm, mix_hbm,
           wc_v, w_v, x_v, xf_v, xt_v, ht_v, a1_v, a2_v, hs_v, pf_v, a_v, out_v, g_v,
           ra_v, rb_v, sa_v, sb_v,
           ag_send, ag_recv, rs_send, rs_recv, ch_send, ch_recv, ld_sem, st_sem):
    p = lax.axis_index("pipe")
    dp = lax.axis_index("dp")
    z, y = dp // NY, lax.rem(dp, NY)

    def dp_at(dz, dy):
        return lax.rem(z + (dz + NZ), NZ) * NY + lax.rem(y + (dy + NY), NY)

    def rows_at(offset):
        return pl.ds(pl.multiple_of(dp_at(offset["z"], offset["y"]) * SHARD, SHARD), SHARD)

    def peer(axis, way):
        return {"dp": dp_at(way, 0) if axis == "z" else dp_at(0, way)}

    is_last, is_first = p == SECTIONS - 1, p == 0

    x_load = pltpu.make_async_copy(x_hbm, x_v, ld_sem.at[0])
    skip_load = pltpu.make_async_copy(skip_hbm, a_v.at[:, SKIP], ld_sem.at[1])
    top_load = pltpu.make_async_copy(top_hbm, a_v.at[:, RES], ld_sem.at[2])
    own = rows_at({"z": 0, "y": 0})
    wc_load = pltpu.make_async_copy(wc_hbm, wc_v, ld_sem.at[3])
    wm_load = pltpu.make_async_copy(wm_hbm, w_v.at[own, CONV:WIDTH], ld_sem.at[4])
    wc_load.start()
    wm_load.start()
    x_load.start()
    skip_load.start()

    @pl.when(is_last)
    def _():
        top_load.start()

    barrier = pltpu.get_barrier_semaphore()
    for axis in ("z", "y"):
        for way in (1, -1):
            pl.semaphore_signal(barrier, inc=1, device_id=peer(axis, way), device_id_type=MESH)

    for way in (1, SECTIONS - 1):
        neighbour = {"pipe": lax.rem(p + way, SECTIONS)}
        pl.semaphore_signal(barrier, inc=1, device_id=neighbour, device_id_type=MESH)
    wc_load.wait()
    taps = wc_v[...].astype(F32)
    for k in range(3):
        w_v[own, k * 1024:(k + 1) * 1024] = taps[:, k, :].astype(BF16)
    wm_load.wait()
    pl.semaphore_wait(barrier, 6)

    ag_sends, ag_order, _ = gather

    def ag_send_copy(ident):
        axis, way, offset, _, piece = ag_sends[ident]
        lanes = slice(piece[0], piece[0] + piece[1])
        here = w_v.at[rows_at(offset), lanes]
        return pltpu.make_async_remote_copy(
            here, here, ag_send.at[ident], ag_recv.at[ident],
            device_id=peer(axis, way), device_id_type=MESH)

    def ag_recv_copy(ident):
        axis, way, _, landed, piece = ag_sends[ident]
        lanes = slice(piece[0], piece[0] + piece[1])
        there = w_v.at[rows_at(landed), lanes]
        return pltpu.make_async_remote_copy(
            there, there, ag_send.at[ident], ag_recv.at[ident],
            device_id=peer(axis, -way), device_id_type=MESH)

    started = False
    for what, ident in ag_order:
        if what == "send":
            ag_send_copy(ident).start()
            continue
        if not started:
            started = True
            x_load.wait()
            for s in range(2):
                xf_v[s * STRIDE:s * STRIDE + PAD, :] = jnp.zeros((PAD, C), F32)
                xf_v[s * STRIDE + PAD:(s + 1) * STRIDE, :] = x_v[s * LEN:(s + 1) * LEN, :].astype(F32)
                pf_v[s * STRIDE + LEN:(s + 1) * STRIDE, :] = jnp.zeros((PAD, 2 * C), F32)
        ag_recv_copy(ident).wait_recv()
    skip_load.wait()

    d = (1 + lax.rem(p, 2)) * (1 + 3 * lax.rem(p // 2, 2)) * (1 + 15 * (p // 4))

    def shifted(ref, base, down):
        window = ref[pl.ds(pl.multiple_of(base, 8), CHUNK + 8), :]
        width = window.shape[1]
        turned = pltpu.roll(window.reshape(CHUNK // 8 + 1, 8, width), down, 1)
        inner = lax.broadcasted_iota(jnp.int32, (CHUNK // 8, 8, width), 1) >= down
        return jnp.where(inner, turned[1:], turned[:-1]).reshape(CHUNK, width).astype(BF16)

    def delayed(s, t, shift):
        down = lax.rem(shift, 8)
        return shifted(xf_v, s * STRIDE + PAD + t - (shift - down) - 8, down)

    def advanced(s, t, shift):
        down = lax.rem(8 - lax.rem(shift, 8), 8)
        return shifted(pf_v, s * STRIDE + t + (shift + down) - 8, down)

    def place(q):
        s = q // PER_SEQ
        t = (PER_SEQ - 1 - lax.rem(q, PER_SEQ)) * CHUNK
        row = pl.multiple_of(s * LEN + t, CHUNK)
        return s, t, pl.ds(row, CHUNK)

    def forward(q):
        s, t, rows = place(q)
        x0 = x_v[rows, :]
        pre = dot(x0, w_v[:, 0:1024])
        pre = pre + dot(delayed(s, t, d), w_v[:, 1024:2048])
        pre = pre + dot(delayed(s, t, 2 * d), w_v[:, 2048:3072])
        filt = jnp.tanh(pre[:, :C])
        gate = jax.nn.sigmoid(pre[:, C:])
        a1_v[rows, :] = gate * (1.0 - filt * filt)
        hid = filt * gate
        a2_v[rows, :] = hid * (1.0 - gate)
        ht_v[:, rows] = hid.astype(BF16).T
        xt_v[:, rows] = x0.T
        hs_v[rows, :] = dot_nt(a_v[rows, SKIP], w_v[:, SKIP])

    def forward_step(q, carry):
        forward(q)
        return carry

    lax.fori_loop(0, jnp.where(is_last, 1, CHUNKS), forward_step, 0)

    @pl.when(is_last)
    def _():
        top_load.wait()

    def chain_send(q):
        _, _, rows = place(q)
        return pltpu.make_async_remote_copy(
            out_v.at[rows, :], a_v.at[rows, RES], ch_send.at[q], ch_recv.at[q],
            device_id={"pipe": p - 1}, device_id_type=MESH)

    def chain_recv(q):
        _, _, rows = place(q)
        return pltpu.make_async_remote_copy(
            a_v.at[rows, RES], a_v.at[rows, RES], ch_send.at[q], ch_recv.at[q],
            device_id={"pipe": p + 1}, device_id_type=MESH)

    def chain_store(q):
        _, _, rows = place(q)
        return pltpu.make_async_copy(out_v.at[rows, :], cot_hbm.at[rows, :], st_sem.at[q])

    def chain_step(q, carry):
        s, t, rows = place(q)

        @pl.when(jnp.logical_not(is_last))
        def _():
            chain_recv(q).wait_recv()

        g = a_v[rows, RES]
        hg = hs_v[rows, :] + dot_nt(g, w_v[:, RES])
        pg1 = (hg * a1_v[rows, :]).astype(BF16)
        pg2 = (hg * a2_v[rows, :]).astype(BF16)
        a_v[rows, 0:C] = pg1
        a_v[rows, C:2 * C] = pg2
        prow = pl.ds(pl.multiple_of(s * STRIDE + t, 8), CHUNK)
        pf_v[prow, 0:C] = pg1.astype(F32)
        pf_v[prow, C:2 * C] = pg2.astype(F32)
        a_v[rows, 1024:2048] = advanced(s, t, d)
        a_v[rows, 2048:3072] = advanced(s, t, 2 * d)
        out = g.astype(F32) + dot_nt(a_v[rows, 0:CONV], w_v[:, 0:CONV])
        out_v[rows, :] = out.astype(BF16)

        @pl.when(jnp.logical_not(is_first))
        def _():
            chain_send(q).start()

        chain_store(q).start()

        @pl.when(jnp.logical_and(is_last, q < CHUNKS - 1))
        def _():
            forward(jnp.minimum(q + 1, CHUNKS - 1))

        return carry

    def grad_step(lhs_v, s, add, n, carry):
        lanes = pl.ds(pl.multiple_of(n * C, C), C)
        rows = slice(s * LEN, (s + 1) * LEN)
        term = dot(lhs_v[:, rows], a_v[rows, lanes])
        g_v[:, lanes] = g_v[:, lanes] + term if add else term
        return carry

    def grads(s, add):
        lax.fori_loop(0, 6, functools.partial(grad_step, xt_v, s, add), 0)
        lax.fori_loop(6, 8, functools.partial(grad_step, ht_v, s, add), 0)

    early = p < 2
    lax.fori_loop(0, PER_SEQ, chain_step, 0)

    @pl.when(early)
    def _():
        grads(0, False)

    lax.fori_loop(PER_SEQ, CHUNKS, chain_step, 0)

    @pl.when(jnp.logical_not(early))
    def _():
        grads(0, False)

    grads(1, True)

    rs_tasks, rs_order, _ = scatter
    starts = (0, RS_SPLIT)
    recv_bufs, send_bufs = (ra_v, rb_v), (sa_v, sb_v)

    def rs_copy(key):
        task = rs_tasks[key]
        group, slot, sem = slots[key]
        lo = task["piece"][0] - starts[group]
        lanes = slice(lo, lo + task["piece"][1])
        source = send_bufs[group].at[slot, :, lanes]
        target = recv_bufs[group].at[slot, :, lanes]
        return pltpu.make_async_remote_copy(
            source, target, rs_send.at[sem], rs_recv.at[sem],
            device_id=peer(task["axis"], task["way"]), device_id_type=MESH)

    def rs_take(key):
        task = rs_tasks[key]
        group, slot, sem = slots[key]
        lo = task["piece"][0] - starts[group]
        view = recv_bufs[group].at[slot, :, lo:lo + task["piece"][1]]
        pltpu.make_async_remote_copy(
            view, view, rs_send.at[sem], rs_recv.at[sem],
            device_id=peer(task["axis"], -task["way"]), device_id_type=MESH).wait_recv()
        return group, slot, task["piece"]

    for key in rs_order:
        task = rs_tasks[key]
        rows = rows_at({"z": task["block"]["z"], "y": task["block"]["y"]})
        first, count = task["piece"]
        got = [rs_take(need) for need in task["recvs"]]
        if task["axis"] is None:
            total = g_v[rows, first:first + count]
            for group, slot, piece in got:
                total = total + recv_bufs[group][slot, :, 0:count].astype(F32)
            g_v[rows, first:first + count] = total
            continue
        group, slot, _ = slots[key]
        base = starts[group]
        spans = [(first, count, None)]
        if got:
            _, have, (p0, pn) = got[0]
            spans = [(p0, pn, have)]
            if p0 > first:
                spans.append((first, p0 - first, None))
            if p0 + pn < first + count:
                spans.append((p0 + pn, first + count - p0 - pn, None))
        for lo, n, have in spans:
            value = g_v[rows, lo:lo + n]
            if have is not None:
                value = value + recv_bufs[group][have, :, lo - base:lo - base + n].astype(F32)
            send_bufs[group][slot, :, lo - base:lo - base + n] = value.astype(BF16)
        rs_copy(key).start()

    own_rows = rows_at({"z": 0, "y": 0})
    grad_stores = [
        pltpu.make_async_copy(
            g_v.at[own_rows, k * 1024:(k + 1) * 1024], conv_hbm.at[k] if k < 3 else mix_hbm, ld_sem.at[k])
        for k in range(4)
    ]
    for store in grad_stores:
        store.start()

    for ident in range(len(ag_sends)):
        ag_send_copy(ident).wait_send()
    for key in rs_order:
        if rs_tasks[key]["axis"] is not None:
            rs_copy(key).wait_send()
    for q in range(CHUNKS):
        chain_store(q).wait()

        @pl.when(jnp.logical_not(is_first))
        def _():
            chain_send(q).wait_send()

    for store in grad_stores:
        store.wait()


def local(x_ckpt, top_cot, skip_cot, w_conv, w_mix):
    x = x_ckpt.reshape(ROWS, C)
    top = top_cot.reshape(ROWS, C)
    skip = skip_cot.reshape(ROWS, C)
    taps = w_conv.reshape(SHARD, 3, 2 * C)
    mix = w_mix.reshape(SHARD, 2 * C)
    gather = gather_plan(AG_SPLIT, WIDTH, SHARD, RATE, LAG)
    scatter = scatter_plan(RS_SPLIT, WIDTH, SHARD, RATE, LAG, 2e-6)
    slots, counts, sems = {}, [0, 0], 0
    for key, task in scatter[0].items():
        if task["axis"] is not None:
            slots[key] = (key[0], counts[key[0]], sems)
            counts[key[0]] += 1
            sems += 1
    sends = len(gather[0])
    anywhere = pl.BlockSpec(memory_space=pl.ANY)
    dma = pltpu.SemaphoreType.DMA
    cot, conv_grad, mix_grad = pl.pallas_call(
        functools.partial(kernel, gather, scatter, slots),
        out_shape=(
            jax.ShapeDtypeStruct((ROWS, C), BF16),
            jax.ShapeDtypeStruct((3, SHARD, 2 * C), F32),
            jax.ShapeDtypeStruct((SHARD, 2 * C), F32),
        ),
        in_specs=[anywhere] * 5,
        out_specs=(anywhere,) * 3,
        scratch_shapes=[
            pltpu.VMEM((SHARD, 3, 2 * C), BF16),
            pltpu.VMEM((C, WIDTH), BF16),
            pltpu.VMEM((ROWS, C), BF16),
            pltpu.VMEM((2 * STRIDE, C), F32),
            pltpu.VMEM((C, ROWS), BF16),
            pltpu.VMEM((C, ROWS), BF16),
            pltpu.VMEM((ROWS, C), F32),
            pltpu.VMEM((ROWS, C), F32),
            pltpu.VMEM((ROWS, C), F32),
            pltpu.VMEM((2 * STRIDE, 2 * C), F32),
            pltpu.VMEM((ROWS, WIDTH), BF16),
            pltpu.VMEM((ROWS, C), BF16),
            pltpu.VMEM((C, WIDTH), F32),
            pltpu.VMEM((counts[0], SHARD, RS_SPLIT), BF16),
            pltpu.VMEM((counts[1], SHARD, WIDTH - RS_SPLIT), BF16),
            pltpu.VMEM((counts[0], SHARD, RS_SPLIT), BF16),
            pltpu.VMEM((counts[1], SHARD, WIDTH - RS_SPLIT), BF16),
            dma((sends,)), dma((sends,)), dma((sems,)), dma((sems,)),
            dma((CHUNKS,)), dma((CHUNKS,)), dma((5,)), dma((CHUNKS,)),
        ],
        compiler_params=pltpu.CompilerParams(
            collective_id=0, has_side_effects=True, vmem_limit_bytes=67043328),
    )(x, top, skip, taps, mix)
    return (
        cot.reshape(x_ckpt.shape),
        conv_grad.transpose(1, 0, 2).reshape(w_conv.shape),
        mix_grad.reshape(w_mix.shape),
    )


def solution(mesh):
    placed = (
        P("pipe", None, "dp", None, None),
        P(None, "dp", None, None),
        P(None, "dp", None, None),
        P("pipe", "dp", None, None),
        P("pipe", "dp", None),
    )
    return jax.shard_map(
        local,
        mesh=mesh,
        in_specs=placed,
        out_specs=(
            P("pipe", None, "dp", None, None),
            P("pipe", "dp", None, None),
            P("pipe", "dp", None),
        ),
        check_vma=False,
    )
```

```python
import functools
import heapq

import jax
import jax.numpy as jnp
from jax import lax
from jax.experimental import pallas as pl
from jax.experimental.pallas import tpu as pltpu
from jax.sharding import PartitionSpec as P

NZ, NY = 8, 4
UNIT = 128


def halves(piece):
    start, count = piece
    first = (count // UNIT + 1) // 2 * UNIT
    return (start, first), (start + first, count - first)


def wrap(offset, count):
    return (offset + count // 2 - 1) % count - (count // 2 - 1)


def gather_plan(split, width, rows, rate, lag):
    sizes = {"z": NZ, "y": NY}
    free, events, sends, order = {}, [], [], []
    seq = 0

    def send(now, group, axis, way, offset, piece):
        nonlocal seq
        if piece[1] == 0:
            return
        key = (axis, way)
        begin = max(now, free.get(key, 0.0))
        free[key] = begin + rows * piece[1] * 2 / rate
        ident = len(sends)
        shift = dict(offset)
        shift[axis] = wrap(shift[axis] - way, sizes[axis])
        sends.append((axis, way, dict(offset), shift, piece))
        order.append(("send", ident))
        heapq.heappush(events, (free[key] + lag, ident, group))
        seq += 1

    axes = (("z", "y"), ("y", "z"))
    pieces = ((0, split), (split, width - split))
    here = {"z": 0, "y": 0}
    for group in (0, 1):
        for way in (1, -1):
            send(0.0, group, axes[group][0], way, here, pieces[group])
    for group in (0, 1):
        for way in (1, -1):
            send(0.0, group, axes[group][1], way, here, pieces[group])
    last = 0.0
    while events:
        now, ident, group = heapq.heappop(events)
        last = now
        axis, way, _, offset, piece = sends[ident]
        order.append(("wait", ident))
        reach = sizes[axis] // 2
        done = abs(offset[axis]) if offset[axis] != reach else reach
        if done < reach - 1:
            send(now, group, axis, way, offset, piece)
        elif done == reach - 1:
            send(now, group, axis, way, offset, halves(piece)[0 if way > 0 else 1])
        if axis == axes[group][0]:
            for side in (1, -1):
                send(now, group, axes[group][1], side, offset, piece)
    return sends, order, last


def scatter_plan(split, width, rows, rate, lag, cost):
    sizes = {"z": NZ, "y": NY}
    axes = (("z", "y"), ("y", "z"))
    pieces = ((0, split), (split, width - split))
    tasks = {}
    for group in (0, 1):
        one, two = axes[group]
        h1, h2 = sizes[one] // 2, sizes[two] // 2
        part1 = halves(pieces[group])
        others = [h2] + [s * j for j in range(h2 - 1, 0, -1) for s in (1, -1)] + [0]
        for rank, o2 in enumerate(others):
            for way in (1, -1):
                for j in range(h1, 0, -1):
                    piece = pieces[group] if j < h1 else part1[0 if way > 0 else 1]
                    needs = [(group, 1, way, j + 1, o2)] if j < h1 else []
                    tasks[(group, 1, way, j, o2)] = dict(
                        axis=one, way=way, block={one: way * j, two: o2}, piece=piece,
                        recvs=needs, locals=[], rank=(rank, -j))
            tasks[(group, 1, 0, 0, o2)] = dict(
                axis=None, way=0, block={one: 0, two: o2}, piece=pieces[group],
                recvs=[(group, 1, 1, 1, o2), (group, 1, -1, 1, o2)], locals=[], rank=(rank, 0))
        for way in (1, -1):
            for j in range(h2, 0, -1):
                piece = pieces[group] if j < h2 else part1[0 if way > 0 else 1]
                needs = [(group, 2, way, j + 1, 0)] if j < h2 else []
                at = way * j if j < h2 else h2
                tasks[(group, 2, way, j, 0)] = dict(
                    axis=two, way=way, block={one: 0, two: at}, piece=piece,
                    recvs=needs, locals=[(group, 1, 0, 0, at)], rank=(-1, -j))
        tasks[(group, 2, 0, 0, 0)] = dict(
            axis=None, way=0, block={one: 0, two: 0}, piece=pieces[group],
            recvs=[(group, 2, 1, 1, 0), (group, 2, -1, 1, 0)], locals=[(group, 1, 0, 0, 0)], rank=(-1, 0))
    arrive, finished, free, order, clock = {}, {}, {}, [], 0.0
    left = dict(tasks)
    while left:
        best = None
        for key, task in left.items():
            if any(n not in arrive for n in task["recvs"]) or any(n not in finished for n in task["locals"]):
                continue
            ready = max([clock] + [arrive[n] for n in task["recvs"]] + [finished[n] for n in task["locals"]])
            link = free.get((task["axis"], task["way"]), 0.0) if task["axis"] else 0.0
            score = (ready, task["rank"], link, key)
            if best is None or score < best[0]:
                best = (score, key, ready)
        _, key, ready = best
        task = left.pop(key)
        clock = ready + cost * rows * task["piece"][1]
        finished[key] = clock
        if task["axis"]:
            lane = (task["axis"], task["way"])
            begin = max(clock, free.get(lane, 0.0))
            free[lane] = begin + rows * task["piece"][1] * 2 / rate
            arrive[key] = free[lane] + lag
        order.append(key)
    return tasks, order, clock


def gather2(split, width, rows, rate, lag, ahead, wts):
    sizes = {"z": NZ, "y": NY}
    axes = (("z", "y"), ("y", "z"))
    pieces = ((0, split), (split, width - split))
    links = {(a, w): [] for a in "zy" for w in (1, -1)}
    free = {k: 0.0 for k in links}
    sends, order, events = [], [], []
    tick = 0
    def offer(now, group, axis, way, offset, piece):
        nonlocal tick
        if piece[1] == 0: return
        reach = sizes[axis] // 2
        gone = abs(offset[axis])
        left = reach - gone
        two = axes[group][1]
        follow = sizes[two] // 2 if axis == axes[group][0] else 0
        score = -(left * wts[0] + follow * wts[1])
        tick += 1
        heapq.heappush(links[(axis, way)], (score, tick, now, group, dict(offset), piece))
    here = {"z": 0, "y": 0}
    for group in (0, 1):
        for axis in axes[group]:
            for way in (1, -1):
                offer(0.0, group, axis, way, here, pieces[group])
    now = 0.0
    last = 0.0
    while True:
        for key, queue in links.items():
            while queue and free[key] <= now + ahead + 1e-6:
                score, _, _, group, offset, piece = heapq.heappop(queue)
                axis, way = key
                begin = max(now, free[key])
                free[key] = begin + rows * piece[1] * 2 / rate
                ident = len(sends)
                shift = dict(offset); shift[axis] = wrap(shift[axis] - way, sizes[axis])
                sends.append((axis, way, dict(offset), shift, piece))
                order.append(("send", ident))
                heapq.heappush(events, (free[key] + lag, 0, ident, group))
        nxt = [free[k] - ahead for k, q in links.items() if q]
        t = min(nxt) if nxt else float("inf")
        if events and events[0][0] <= t:
            now, _, ident, group = heapq.heappop(events)
            last = max(last, now)
            axis, way, _, offset, piece = sends[ident]
            order.append(("wait", ident))
            reach = sizes[axis] // 2
            done = abs(offset[axis])
            if done < reach - 1: offer(now, group, axis, way, offset, piece)
            elif done == reach - 1: offer(now, group, axis, way, offset, halves(piece)[0 if way > 0 else 1])
            if axis == axes[group][0]:
                for side in (1, -1): offer(now, group, axes[group][1], side, offset, piece)
        elif nxt:
            now = max(now, t)
        else:
            break
    return sends, order, last


def scatter2(split, width, rows, rate, lag, cost, ahead, wts):
    tasks = scatter_plan(split, width, rows, rate, lag, cost)[0]
    needs, users = {}, {}
    for key, task in tasks.items():
        deps = [("r", n) for n in task["recvs"]] + [("l", n) for n in task["locals"]]
        needs[key] = len(deps)
        for kind, n in deps:
            users.setdefault((kind, n), []).append(key)
    links = {(a, w): [] for a in "zy" for w in (1, -1)}
    free = {k: 0.0 for k in links}
    order, events = [], []
    def remaining(key):
        group, stage, way, j, o2 = key
        return wts[0] * j + wts[1] * abs(o2) * (stage == 1)
    def ready(key, now):
        task = tasks[key]
        if task["axis"] is None:
            order.append(key)
            heapq.heappush(events, (now + cost * rows * task["piece"][1], "l", key))
        else:
            heapq.heappush(links[(task["axis"], task["way"])], (-remaining(key), len(order), key))
    now = 0.0
    for key in tasks:
        if needs[key] == 0: ready(key, 0.0)
    last = 0.0
    while True:
        for link, queue in links.items():
            while queue and free[link] <= now + ahead + 1e-6:
                key = heapq.heappop(queue)[2]
                begin = max(now, free[link])
                free[link] = begin + rows * tasks[key]["piece"][1] * 2 / rate
                order.append(key)
                heapq.heappush(events, (free[link] + lag, "r", key))
        nxt = [free[k] - ahead for k, q in links.items() if q]
        t = min(nxt) if nxt else float("inf")
        if events and events[0][0] <= t:
            now, kind, key = heapq.heappop(events)
            last = max(last, now)
            for user in users.get((kind, key), []):
                needs[user] -= 1
                if needs[user] == 0: ready(user, now)
        elif nxt:
            now = max(now, t)
        else:
            break
    assert len(order) == len(tasks)
    return tasks, order, last


F32, BF16 = jnp.float32, jnp.bfloat16
MESH = pl.DeviceIdType.MESH
SECTIONS = 8
C = 512
LEN = 512
ROWS = 1024
SHARD = 16
WIDTH = 4096
CONV = 3072
RES = slice(3072, 3584)
SKIP = slice(3584, 4096)
CHUNK = 256
CHUNKS = ROWS // CHUNK
PER_SEQ = LEN // CHUNK
PAD = 264
STRIDE = LEN + PAD
RATE, LAG = 46.5e3, 1.8
AG_SPLIT, RS_SPLIT = 2560, 1536
NT = (((1,), (1,)), ((), ()))


def dot(a, b):
    return jnp.dot(a, b, preferred_element_type=F32)


def dot_nt(a, b):
    return lax.dot_general(a, b, NT, preferred_element_type=F32)


def kernel(gather, scatter, slots, x_hbm, top_hbm, skip_hbm, wc_hbm, wm_hbm, cot_hbm, conv_hbm, mix_hbm,
           w_v, x_v, xf_v, xt_v, ht_v, a1_v, a2_v, hs_v, pf_v, a_v, out_v, g_v,
           ra_v, rb_v, sa_v, sb_v,
           ag_send, ag_recv, rs_send, rs_recv, ch_send, ch_recv, ld_sem, st_sem):
    p = lax.axis_index("pipe")
    dp = lax.axis_index("dp")
    z, y = dp // NY, lax.rem(dp, NY)

    def dp_at(dz, dy):
        return lax.rem(z + (dz + NZ), NZ) * NY + lax.rem(y + (dy + NY), NY)

    def rows_at(offset):
        return pl.ds(pl.multiple_of(dp_at(offset["z"], offset["y"]) * SHARD, SHARD), SHARD)

    def peer(axis, way):
        return {"dp": dp_at(way, 0) if axis == "z" else dp_at(0, way)}

    is_last, is_first = p == SECTIONS - 1, p == 0

    x_load = pltpu.make_async_copy(x_hbm, x_v, ld_sem.at[0])
    skip_load = pltpu.make_async_copy(skip_hbm, a_v.at[:, SKIP], ld_sem.at[1])
    top_load = pltpu.make_async_copy(top_hbm, a_v.at[:, RES], ld_sem.at[2])
    own = rows_at({"z": 0, "y": 0})
    own_loads = [
        pltpu.make_async_copy(
            wc_hbm.at[k] if k < 3 else wm_hbm, w_v.at[own, k * 1024:(k + 1) * 1024], ld_sem.at[3 + k])
        for k in range(4)
    ]
    for load in own_loads:
        load.start()
    x_load.start()
    skip_load.start()

    @pl.when(is_last)
    def _():
        top_load.start()

    barrier = pltpu.get_barrier_semaphore()
    for axis in ("z", "y"):
        for way in (1, -1):
            pl.semaphore_signal(barrier, inc=1, device_id=peer(axis, way), device_id_type=MESH)

    for way in (1, SECTIONS - 1):
        neighbour = {"pipe": lax.rem(p + way, SECTIONS)}
        pl.semaphore_signal(barrier, inc=1, device_id=neighbour, device_id_type=MESH)
    for load in own_loads:
        load.wait()
    pl.semaphore_wait(barrier, 6)

    ag_sends, ag_order, _ = gather

    def ag_send_copy(ident):
        axis, way, offset, _, piece = ag_sends[ident]
        lanes = slice(piece[0], piece[0] + piece[1])
        here = w_v.at[rows_at(offset), lanes]
        return pltpu.make_async_remote_copy(
            here, here, ag_send.at[ident], ag_recv.at[ident],
            device_id=peer(axis, way), device_id_type=MESH)

    def ag_recv_copy(ident):
        axis, way, _, landed, piece = ag_sends[ident]
        lanes = slice(piece[0], piece[0] + piece[1])
        there = w_v.at[rows_at(landed), lanes]
        return pltpu.make_async_remote_copy(
            there, there, ag_send.at[ident], ag_recv.at[ident],
            device_id=peer(axis, -way), device_id_type=MESH)

    started = False
    for what, ident in ag_order:
        if what == "send":
            ag_send_copy(ident).start()
            continue
        if not started:
            started = True
            x_load.wait()
            for s in range(2):
                xf_v[s * STRIDE:s * STRIDE + PAD, :] = jnp.zeros((PAD, C), F32)
                xf_v[s * STRIDE + PAD:(s + 1) * STRIDE, :] = x_v[s * LEN:(s + 1) * LEN, :].astype(F32)
                pf_v[s * STRIDE + LEN:(s + 1) * STRIDE, :] = jnp.zeros((PAD, 2 * C), F32)
        ag_recv_copy(ident).wait_recv()
    skip_load.wait()

    d = (1 + lax.rem(p, 2)) * (1 + 3 * lax.rem(p // 2, 2)) * (1 + 15 * (p // 4))

    def shifted(ref, base, down):
        window = ref[pl.ds(pl.multiple_of(base, 8), CHUNK + 8), :]
        width = window.shape[1]
        turned = pltpu.roll(window.reshape(CHUNK // 8 + 1, 8, width), down, 1)
        inner = lax.broadcasted_iota(jnp.int32, (CHUNK // 8, 8, width), 1) >= down
        return jnp.where(inner, turned[1:], turned[:-1]).reshape(CHUNK, width).astype(BF16)

    def delayed(s, t, shift):
        down = lax.rem(shift, 8)
        return shifted(xf_v, s * STRIDE + PAD + t - (shift - down) - 8, down)

    def advanced(s, t, shift):
        down = lax.rem(8 - lax.rem(shift, 8), 8)
        return shifted(pf_v, s * STRIDE + t + (shift + down) - 8, down)

    def place(q):
        s = q // PER_SEQ
        t = (PER_SEQ - 1 - lax.rem(q, PER_SEQ)) * CHUNK
        row = pl.multiple_of(s * LEN + t, CHUNK)
        return s, t, pl.ds(row, CHUNK)

    def forward(q):
        s, t, rows = place(q)
        x0 = x_v[rows, :]
        pre = dot(x0, w_v[:, 0:1024])
        pre = pre + dot(delayed(s, t, d), w_v[:, 1024:2048])
        pre = pre + dot(delayed(s, t, 2 * d), w_v[:, 2048:3072])
        filt = jnp.tanh(pre[:, :C])
        gate = jax.nn.sigmoid(pre[:, C:])
        a1_v[rows, :] = gate * (1.0 - filt * filt)
        hid = filt * gate
        a2_v[rows, :] = hid * (1.0 - gate)
        ht_v[:, rows] = hid.astype(BF16).T
        xt_v[:, rows] = x0.T
        hs_v[rows, :] = dot_nt(a_v[rows, SKIP], w_v[:, SKIP])

    def forward_step(q, carry):
        forward(q)
        return carry

    lax.fori_loop(0, jnp.where(is_last, 1, CHUNKS), forward_step, 0)

    @pl.when(is_last)
    def _():
        top_load.wait()

    def chain_send(q):
        _, _, rows = place(q)
        return pltpu.make_async_remote_copy(
            out_v.at[rows, :], a_v.at[rows, RES], ch_send.at[q], ch_recv.at[q],
            device_id={"pipe": p - 1}, device_id_type=MESH)

    def chain_recv(q):
        _, _, rows = place(q)
        return pltpu.make_async_remote_copy(
            a_v.at[rows, RES], a_v.at[rows, RES], ch_send.at[q], ch_recv.at[q],
            device_id={"pipe": p + 1}, device_id_type=MESH)

    def chain_store(q):
        _, _, rows = place(q)
        return pltpu.make_async_copy(out_v.at[rows, :], cot_hbm.at[rows, :], st_sem.at[q])

    def chain_step(q, carry):
        s, t, rows = place(q)

        @pl.when(jnp.logical_not(is_last))
        def _():
            chain_recv(q).wait_recv()

        g = a_v[rows, RES]
        hg = hs_v[rows, :] + dot_nt(g, w_v[:, RES])
        pg1 = (hg * a1_v[rows, :]).astype(BF16)
        pg2 = (hg * a2_v[rows, :]).astype(BF16)
        a_v[rows, 0:C] = pg1
        a_v[rows, C:2 * C] = pg2
        prow = pl.ds(pl.multiple_of(s * STRIDE + t, 8), CHUNK)
        pf_v[prow, 0:C] = pg1.astype(F32)
        pf_v[prow, C:2 * C] = pg2.astype(F32)
        a_v[rows, 1024:2048] = advanced(s, t, d)
        a_v[rows, 2048:3072] = advanced(s, t, 2 * d)
        out = g.astype(F32) + dot_nt(a_v[rows, 0:CONV], w_v[:, 0:CONV])
        out_v[rows, :] = out.astype(BF16)

        @pl.when(jnp.logical_not(is_first))
        def _():
            chain_send(q).start()

        chain_store(q).start()

        @pl.when(jnp.logical_and(is_last, q < CHUNKS - 1))
        def _():
            forward(jnp.minimum(q + 1, CHUNKS - 1))

        return carry

    def grad_step(lhs_v, s, add, n, carry):
        lanes = pl.ds(pl.multiple_of(n * C, C), C)
        rows = slice(s * LEN, (s + 1) * LEN)
        term = dot(lhs_v[:, rows], a_v[rows, lanes])
        g_v[:, lanes] = g_v[:, lanes] + term if add else term
        return carry

    def grads(s, add):
        lax.fori_loop(0, 6, functools.partial(grad_step, xt_v, s, add), 0)
        lax.fori_loop(6, 8, functools.partial(grad_step, ht_v, s, add), 0)

    early = p < 2
    lax.fori_loop(0, PER_SEQ, chain_step, 0)

    @pl.when(early)
    def _():
        grads(0, False)

    lax.fori_loop(PER_SEQ, CHUNKS, chain_step, 0)

    @pl.when(jnp.logical_not(early))
    def _():
        grads(0, False)

    grads(1, True)

    rs_tasks, rs_order, _ = scatter
    starts = (0, RS_SPLIT)
    recv_bufs, send_bufs = (ra_v, rb_v), (sa_v, sb_v)

    def rs_copy(key):
        task = rs_tasks[key]
        group, slot, sem = slots[key]
        lo = task["piece"][0] - starts[group]
        lanes = slice(lo, lo + task["piece"][1])
        source = send_bufs[group].at[slot, :, lanes]
        target = recv_bufs[group].at[slot, :, lanes]
        return pltpu.make_async_remote_copy(
            source, target, rs_send.at[sem], rs_recv.at[sem],
            device_id=peer(task["axis"], task["way"]), device_id_type=MESH)

    def rs_take(key):
        task = rs_tasks[key]
        group, slot, sem = slots[key]
        lo = task["piece"][0] - starts[group]
        view = recv_bufs[group].at[slot, :, lo:lo + task["piece"][1]]
        pltpu.make_async_remote_copy(
            view, view, rs_send.at[sem], rs_recv.at[sem],
            device_id=peer(task["axis"], -task["way"]), device_id_type=MESH).wait_recv()
        return group, slot, task["piece"]

    for key in rs_order:
        task = rs_tasks[key]
        rows = rows_at({"z": task["block"]["z"], "y": task["block"]["y"]})
        first, count = task["piece"]
        got = [rs_take(need) for need in task["recvs"]]
        if task["axis"] is None:
            total = g_v[rows, first:first + count]
            for group, slot, piece in got:
                total = total + recv_bufs[group][slot, :, 0:count].astype(F32)
            g_v[rows, first:first + count] = total
            continue
        group, slot, _ = slots[key]
        base = starts[group]
        spans = [(first, count, None)]
        if got:
            _, have, (p0, pn) = got[0]
            spans = [(p0, pn, have)]
            if p0 > first:
                spans.append((first, p0 - first, None))
            if p0 + pn < first + count:
                spans.append((p0 + pn, first + count - p0 - pn, None))
        for lo, n, have in spans:
            value = g_v[rows, lo:lo + n]
            if have is not None:
                value = value + recv_bufs[group][have, :, lo - base:lo - base + n].astype(F32)
            send_bufs[group][slot, :, lo - base:lo - base + n] = value.astype(BF16)
        rs_copy(key).start()

    own_rows = rows_at({"z": 0, "y": 0})
    grad_stores = [
        pltpu.make_async_copy(
            g_v.at[own_rows, k * 1024:(k + 1) * 1024], conv_hbm.at[k] if k < 3 else mix_hbm, ld_sem.at[k])
        for k in range(4)
    ]
    for store in grad_stores:
        store.start()

    for ident in range(len(ag_sends)):
        ag_send_copy(ident).wait_send()
    for key in rs_order:
        if rs_tasks[key]["axis"] is not None:
            rs_copy(key).wait_send()
    for q in range(CHUNKS):
        chain_store(q).wait()

        @pl.when(jnp.logical_not(is_first))
        def _():
            chain_send(q).wait_send()

    for store in grad_stores:
        store.wait()


def local(x_ckpt, top_cot, skip_cot, w_conv, w_mix):
    x = x_ckpt.reshape(ROWS, C)
    top = top_cot.reshape(ROWS, C)
    skip = skip_cot.reshape(ROWS, C)
    taps = w_conv.reshape(SHARD, 3, 2 * C).transpose(1, 0, 2)
    mix = w_mix.reshape(SHARD, 2 * C)
    gather = gather2(AG_SPLIT, WIDTH, SHARD, 53e3, 2.4, 0.0, (1, 1))
    scatter = scatter2(RS_SPLIT, WIDTH, SHARD, 53e3, 2.4, 2e-6, 0.0, (1, 1))
    slots, counts, sems = {}, [0, 0], 0
    for key, task in scatter[0].items():
        if task["axis"] is not None:
            slots[key] = (key[0], counts[key[0]], sems)
            counts[key[0]] += 1
            sems += 1
    sends = len(gather[0])
    anywhere = pl.BlockSpec(memory_space=pl.ANY)
    dma = pltpu.SemaphoreType.DMA
    cot, conv_grad, mix_grad = pl.pallas_call(
        functools.partial(kernel, gather, scatter, slots),
        out_shape=(
            jax.ShapeDtypeStruct((ROWS, C), BF16),
            jax.ShapeDtypeStruct((3, SHARD, 2 * C), F32),
            jax.ShapeDtypeStruct((SHARD, 2 * C), F32),
        ),
        in_specs=[anywhere] * 5,
        out_specs=(anywhere,) * 3,
        scratch_shapes=[
            pltpu.VMEM((C, WIDTH), BF16),
            pltpu.VMEM((ROWS, C), BF16),
            pltpu.VMEM((2 * STRIDE, C), F32),
            pltpu.VMEM((C, ROWS), BF16),
            pltpu.VMEM((C, ROWS), BF16),
            pltpu.VMEM((ROWS, C), F32),
            pltpu.VMEM((ROWS, C), F32),
            pltpu.VMEM((ROWS, C), F32),
            pltpu.VMEM((2 * STRIDE, 2 * C), F32),
            pltpu.VMEM((ROWS, WIDTH), BF16),
            pltpu.VMEM((ROWS, C), BF16),
            pltpu.VMEM((C, WIDTH), F32),
            pltpu.VMEM((counts[0], SHARD, RS_SPLIT), BF16),
            pltpu.VMEM((counts[1], SHARD, WIDTH - RS_SPLIT), BF16),
            pltpu.VMEM((counts[0], SHARD, RS_SPLIT), BF16),
            pltpu.VMEM((counts[1], SHARD, WIDTH - RS_SPLIT), BF16),
            dma((sends,)), dma((sends,)), dma((sems,)), dma((sems,)),
            dma((CHUNKS,)), dma((CHUNKS,)), dma((7,)), dma((CHUNKS,)),
        ],
        compiler_params=pltpu.CompilerParams(
            collective_id=0, has_side_effects=True, vmem_limit_bytes=67043328),
    )(x, top, skip, taps, mix)
    return (
        cot.reshape(x_ckpt.shape),
        conv_grad.transpose(1, 0, 2).reshape(w_conv.shape),
        mix_grad.reshape(w_mix.shape),
    )


def solution(mesh):
    placed = (
        P("pipe", None, "dp", None, None),
        P(None, "dp", None, None),
        P(None, "dp", None, None),
        P("pipe", "dp", None, None),
        P("pipe", "dp", None),
    )
    return jax.shard_map(
        local,
        mesh=mesh,
        in_specs=placed,
        out_specs=(
            P("pipe", None, "dp", None, None),
            P("pipe", "dp", None, None),
            P("pipe", "dp", None),
        ),
        check_vma=False,
    )
```

```python
import functools
import heapq

import jax
import jax.numpy as jnp
from jax import lax
from jax.experimental import pallas as pl
from jax.experimental.pallas import tpu as pltpu
from jax.sharding import PartitionSpec as P

NZ, NY = 8, 4
UNIT = 128


def halves(piece):
    start, count = piece
    first = (count // UNIT + 1) // 2 * UNIT
    return (start, first), (start + first, count - first)


def wrap(offset, count):
    return (offset + count // 2 - 1) % count - (count // 2 - 1)


def gather_plan(split, width, rows, rate, lag):
    sizes = {"z": NZ, "y": NY}
    free, events, sends, order = {}, [], [], []
    seq = 0

    def send(now, group, axis, way, offset, piece):
        nonlocal seq
        if piece[1] == 0:
            return
        key = (axis, way)
        begin = max(now, free.get(key, 0.0))
        free[key] = begin + rows * piece[1] * 2 / rate
        ident = len(sends)
        shift = dict(offset)
        shift[axis] = wrap(shift[axis] - way, sizes[axis])
        sends.append((axis, way, dict(offset), shift, piece))
        order.append(("send", ident))
        heapq.heappush(events, (free[key] + lag, ident, group))
        seq += 1

    axes = (("z", "y"), ("y", "z"))
    pieces = ((0, split), (split, width - split))
    here = {"z": 0, "y": 0}
    for group in (0, 1):
        for way in (1, -1):
            send(0.0, group, axes[group][0], way, here, pieces[group])
    for group in (0, 1):
        for way in (1, -1):
            send(0.0, group, axes[group][1], way, here, pieces[group])
    last = 0.0
    while events:
        now, ident, group = heapq.heappop(events)
        last = now
        axis, way, _, offset, piece = sends[ident]
        order.append(("wait", ident))
        reach = sizes[axis] // 2
        done = abs(offset[axis]) if offset[axis] != reach else reach
        if done < reach - 1:
            send(now, group, axis, way, offset, piece)
        elif done == reach - 1:
            send(now, group, axis, way, offset, halves(piece)[0 if way > 0 else 1])
        if axis == axes[group][0]:
            for side in (1, -1):
                send(now, group, axes[group][1], side, offset, piece)
    return sends, order, last


def scatter_plan(split, width, rows, rate, lag, cost):
    sizes = {"z": NZ, "y": NY}
    axes = (("z", "y"), ("y", "z"))
    pieces = ((0, split), (split, width - split))
    tasks = {}
    for group in (0, 1):
        one, two = axes[group]
        h1, h2 = sizes[one] // 2, sizes[two] // 2
        part1 = halves(pieces[group])
        others = [h2] + [s * j for j in range(h2 - 1, 0, -1) for s in (1, -1)] + [0]
        for rank, o2 in enumerate(others):
            for way in (1, -1):
                for j in range(h1, 0, -1):
                    piece = pieces[group] if j < h1 else part1[0 if way > 0 else 1]
                    needs = [(group, 1, way, j + 1, o2)] if j < h1 else []
                    tasks[(group, 1, way, j, o2)] = dict(
                        axis=one, way=way, block={one: way * j, two: o2}, piece=piece,
                        recvs=needs, locals=[], rank=(rank, -j))
            tasks[(group, 1, 0, 0, o2)] = dict(
                axis=None, way=0, block={one: 0, two: o2}, piece=pieces[group],
                recvs=[(group, 1, 1, 1, o2), (group, 1, -1, 1, o2)], locals=[], rank=(rank, 0))
        for way in (1, -1):
            for j in range(h2, 0, -1):
                piece = pieces[group] if j < h2 else part1[0 if way > 0 else 1]
                needs = [(group, 2, way, j + 1, 0)] if j < h2 else []
                at = way * j if j < h2 else h2
                tasks[(group, 2, way, j, 0)] = dict(
                    axis=two, way=way, block={one: 0, two: at}, piece=piece,
                    recvs=needs, locals=[(group, 1, 0, 0, at)], rank=(-1, -j))
        tasks[(group, 2, 0, 0, 0)] = dict(
            axis=None, way=0, block={one: 0, two: 0}, piece=pieces[group],
            recvs=[(group, 2, 1, 1, 0), (group, 2, -1, 1, 0)], locals=[(group, 1, 0, 0, 0)], rank=(-1, 0))
    arrive, finished, free, order, clock = {}, {}, {}, [], 0.0
    left = dict(tasks)
    while left:
        best = None
        for key, task in left.items():
            if any(n not in arrive for n in task["recvs"]) or any(n not in finished for n in task["locals"]):
                continue
            ready = max([clock] + [arrive[n] for n in task["recvs"]] + [finished[n] for n in task["locals"]])
            link = free.get((task["axis"], task["way"]), 0.0) if task["axis"] else 0.0
            score = (ready, task["rank"], link, key)
            if best is None or score < best[0]:
                best = (score, key, ready)
        _, key, ready = best
        task = left.pop(key)
        clock = ready + cost * rows * task["piece"][1]
        finished[key] = clock
        if task["axis"]:
            lane = (task["axis"], task["way"])
            begin = max(clock, free.get(lane, 0.0))
            free[lane] = begin + rows * task["piece"][1] * 2 / rate
            arrive[key] = free[lane] + lag
        order.append(key)
    return tasks, order, clock


def gather2(split, width, rows, rate, lag, ahead, wts):
    sizes = {"z": NZ, "y": NY}
    axes = (("z", "y"), ("y", "z"))
    pieces = ((0, split), (split, width - split))
    links = {(a, w): [] for a in "zy" for w in (1, -1)}
    free = {k: 0.0 for k in links}
    sends, order, events = [], [], []
    tick = 0
    def offer(now, group, axis, way, offset, piece):
        nonlocal tick
        if piece[1] == 0: return
        reach = sizes[axis] // 2
        gone = abs(offset[axis])
        left = reach - gone
        two = axes[group][1]
        follow = sizes[two] // 2 if axis == axes[group][0] else 0
        score = -(left * wts[0] + follow * wts[1])
        tick += 1
        heapq.heappush(links[(axis, way)], (score, tick, now, group, dict(offset), piece))
    here = {"z": 0, "y": 0}
    for group in (0, 1):
        for axis in axes[group]:
            for way in (1, -1):
                offer(0.0, group, axis, way, here, pieces[group])
    now = 0.0
    last = 0.0
    while True:
        for key, queue in links.items():
            while queue and free[key] <= now + ahead + 1e-6:
                score, _, _, group, offset, piece = heapq.heappop(queue)
                axis, way = key
                begin = max(now, free[key])
                free[key] = begin + rows * piece[1] * 2 / rate
                ident = len(sends)
                shift = dict(offset); shift[axis] = wrap(shift[axis] - way, sizes[axis])
                sends.append((axis, way, dict(offset), shift, piece))
                order.append(("send", ident))
                heapq.heappush(events, (free[key] + lag, 0, ident, group))
        nxt = [free[k] - ahead for k, q in links.items() if q]
        t = min(nxt) if nxt else float("inf")
        if events and events[0][0] <= t:
            now, _, ident, group = heapq.heappop(events)
            last = max(last, now)
            axis, way, _, offset, piece = sends[ident]
            order.append(("wait", ident))
            reach = sizes[axis] // 2
            done = abs(offset[axis])
            if done < reach - 1: offer(now, group, axis, way, offset, piece)
            elif done == reach - 1: offer(now, group, axis, way, offset, halves(piece)[0 if way > 0 else 1])
            if axis == axes[group][0]:
                for side in (1, -1): offer(now, group, axes[group][1], side, offset, piece)
        elif nxt:
            now = max(now, t)
        else:
            break
    return sends, order, last


def scatter2(split, width, rows, rate, lag, cost, ahead, wts):
    tasks = scatter_plan(split, width, rows, rate, lag, cost)[0]
    needs, users = {}, {}
    for key, task in tasks.items():
        deps = [("r", n) for n in task["recvs"]] + [("l", n) for n in task["locals"]]
        needs[key] = len(deps)
        for kind, n in deps:
            users.setdefault((kind, n), []).append(key)
    links = {(a, w): [] for a in "zy" for w in (1, -1)}
    free = {k: 0.0 for k in links}
    order, events = [], []
    def remaining(key):
        group, stage, way, j, o2 = key
        return wts[0] * j + wts[1] * abs(o2) * (stage == 1)
    def ready(key, now):
        task = tasks[key]
        if task["axis"] is None:
            order.append(key)
            heapq.heappush(events, (now + cost * rows * task["piece"][1], "l", key))
        else:
            heapq.heappush(links[(task["axis"], task["way"])], (-remaining(key), len(order), key))
    now = 0.0
    for key in tasks:
        if needs[key] == 0: ready(key, 0.0)
    last = 0.0
    while True:
        for link, queue in links.items():
            while queue and free[link] <= now + ahead + 1e-6:
                key = heapq.heappop(queue)[2]
                begin = max(now, free[link])
                free[link] = begin + rows * tasks[key]["piece"][1] * 2 / rate
                order.append(key)
                heapq.heappush(events, (free[link] + lag, "r", key))
        nxt = [free[k] - ahead for k, q in links.items() if q]
        t = min(nxt) if nxt else float("inf")
        if events and events[0][0] <= t:
            now, kind, key = heapq.heappop(events)
            last = max(last, now)
            for user in users.get((kind, key), []):
                needs[user] -= 1
                if needs[user] == 0: ready(user, now)
        elif nxt:
            now = max(now, t)
        else:
            break
    assert len(order) == len(tasks)
    return tasks, order, last


F32, BF16 = jnp.float32, jnp.bfloat16
MESH = pl.DeviceIdType.MESH
SECTIONS = 8
C = 512
LEN = 512
ROWS = 1024
SHARD = 16
WIDTH = 4096
CONV = 3072
RES = slice(3072, 3584)
SKIP = slice(3584, 4096)
CHUNK = 128
AHEAD = 256
CHUNKS = ROWS // CHUNK
AHEADS = ROWS // AHEAD
RATIO = AHEAD // CHUNK
PER_SEQ = LEN // CHUNK
PAD = 264
STRIDE = LEN + PAD
RATE, LAG = 46.5e3, 1.8
AG_SPLIT, RS_SPLIT = 2560, 1536
NT = (((1,), (1,)), ((), ()))


def dot(a, b):
    return jnp.dot(a, b, preferred_element_type=F32)


def dot_nt(a, b):
    return lax.dot_general(a, b, NT, preferred_element_type=F32)


def kernel(gather, scatter, slots, x_hbm, top_hbm, skip_hbm, wc_hbm, wm_hbm, cot_hbm, conv_hbm, mix_hbm,
           w_v, wt_v, x_v, xf_v, xt_v, ht_v, a1_v, a2_v, hs_v, pf_v, a_v, out_v, g_v,
           ra_v, rb_v, sa_v, sb_v,
           ag_send, ag_recv, rs_send, rs_recv, ch_send, ch_recv, ld_sem, st_sem):
    p = lax.axis_index("pipe")
    dp = lax.axis_index("dp")
    z, y = dp // NY, lax.rem(dp, NY)

    def dp_at(dz, dy):
        return lax.rem(z + (dz + NZ), NZ) * NY + lax.rem(y + (dy + NY), NY)

    def rows_at(offset):
        return pl.ds(pl.multiple_of(dp_at(offset["z"], offset["y"]) * SHARD, SHARD), SHARD)

    def peer(axis, way):
        return {"dp": dp_at(way, 0) if axis == "z" else dp_at(0, way)}

    is_last, is_first = p == SECTIONS - 1, p == 0

    x_load = pltpu.make_async_copy(x_hbm, x_v, ld_sem.at[0])
    skip_load = pltpu.make_async_copy(skip_hbm, a_v.at[:, SKIP], ld_sem.at[1])
    top_load = pltpu.make_async_copy(top_hbm, a_v.at[:, RES], ld_sem.at[2])
    own = rows_at({"z": 0, "y": 0})
    own_loads = [
        pltpu.make_async_copy(
            wc_hbm.at[k] if k < 3 else wm_hbm, w_v.at[own, k * 1024:(k + 1) * 1024], ld_sem.at[3 + k])
        for k in range(4)
    ]
    for load in own_loads:
        load.start()
    x_load.start()
    skip_load.start()

    @pl.when(is_last)
    def _():
        top_load.start()

    barrier = pltpu.get_barrier_semaphore()
    for axis in ("z", "y"):
        for way in (1, -1):
            pl.semaphore_signal(barrier, inc=1, device_id=peer(axis, way), device_id_type=MESH)

    for way in (1, SECTIONS - 1):
        neighbour = {"pipe": lax.rem(p + way, SECTIONS)}
        pl.semaphore_signal(barrier, inc=1, device_id=neighbour, device_id_type=MESH)
    for load in own_loads:
        load.wait()
    pl.semaphore_wait(barrier, 6)

    ag_sends, ag_order, _ = gather

    def ag_send_copy(ident):
        axis, way, offset, _, piece = ag_sends[ident]
        lanes = slice(piece[0], piece[0] + piece[1])
        here = w_v.at[rows_at(offset), lanes]
        return pltpu.make_async_remote_copy(
            here, here, ag_send.at[ident], ag_recv.at[ident],
            device_id=peer(axis, way), device_id_type=MESH)

    def ag_recv_copy(ident):
        axis, way, _, landed, piece = ag_sends[ident]
        lanes = slice(piece[0], piece[0] + piece[1])
        there = w_v.at[rows_at(landed), lanes]
        return pltpu.make_async_remote_copy(
            there, there, ag_send.at[ident], ag_recv.at[ident],
            device_id=peer(axis, -way), device_id_type=MESH)

    started = False
    for what, ident in ag_order:
        if what == "send":
            ag_send_copy(ident).start()
            continue
        if not started:
            started = True
            x_load.wait()
            for s in range(2):
                xf_v[s * STRIDE:s * STRIDE + PAD, :] = jnp.zeros((PAD, C), F32)
                xf_v[s * STRIDE + PAD:(s + 1) * STRIDE, :] = x_v[s * LEN:(s + 1) * LEN, :].astype(F32)
                pf_v[s * STRIDE + LEN:(s + 1) * STRIDE, :] = jnp.zeros((PAD, 2 * C), F32)
        ag_recv_copy(ident).wait_recv()
    skip_load.wait()

    d = (1 + lax.rem(p, 2)) * (1 + 3 * lax.rem(p // 2, 2)) * (1 + 15 * (p // 4))

    def shifted(ref, base, down, size):
        window = ref[pl.ds(pl.multiple_of(base, 8), size + 8), :]
        width = window.shape[1]
        turned = pltpu.roll(window.reshape(size // 8 + 1, 8, width), down, 1)
        inner = lax.broadcasted_iota(jnp.int32, (size // 8, 8, width), 1) >= down
        return jnp.where(inner, turned[1:], turned[:-1]).reshape(size, width).astype(BF16)

    def delayed(s, t, shift):
        down = lax.rem(shift, 8)
        return shifted(xf_v, s * STRIDE + PAD + t - (shift - down) - 8, down, AHEAD)

    def advanced(s, t, shift):
        down = lax.rem(8 - lax.rem(shift, 8), 8)
        return shifted(pf_v, s * STRIDE + t + (shift + down) - 8, down, CHUNK)

    def place(q, size):
        per = LEN // size
        s = q // per
        t = (per - 1 - lax.rem(q, per)) * size
        row = pl.multiple_of(s * LEN + t, size)
        return s, t, pl.ds(row, size)

    def forward(q):
        s, t, rows = place(q, AHEAD)
        x0 = x_v[rows, :]
        pre = dot(x0, w_v[:, 0:1024])
        pre = pre + dot(delayed(s, t, d), w_v[:, 1024:2048])
        pre = pre + dot(delayed(s, t, 2 * d), w_v[:, 2048:3072])
        filt = jnp.tanh(pre[:, :C])
        gate = jax.nn.sigmoid(pre[:, C:])
        a1_v[rows, :] = gate * (1.0 - filt * filt)
        hid = filt * gate
        a2_v[rows, :] = hid * (1.0 - gate)
        ht_v[:, rows] = hid.astype(BF16).T
        xt_v[:, rows] = x0.T
        hs_v[rows, :] = dot_nt(a_v[rows, SKIP], w_v[:, SKIP])

    def forward_step(q, carry):
        forward(q)
        return carry

    lax.fori_loop(0, jnp.where(is_last, 1, AHEADS), forward_step, 0)

    def turn_step(n, carry):
        lanes = pl.ds(pl.multiple_of(n * C, C), C)
        wt_v[lanes, :] = w_v[:, lanes].T
        return carry

    lax.fori_loop(0, (CONV + C) // C, turn_step, 0)

    @pl.when(is_last)
    def _():
        top_load.wait()

    def chain_send(q):
        _, _, rows = place(q, CHUNK)
        return pltpu.make_async_remote_copy(
            out_v.at[rows, :], a_v.at[rows, RES], ch_send.at[q], ch_recv.at[q],
            device_id={"pipe": p - 1}, device_id_type=MESH)

    def chain_recv(q):
        _, _, rows = place(q, CHUNK)
        return pltpu.make_async_remote_copy(
            a_v.at[rows, RES], a_v.at[rows, RES], ch_send.at[q], ch_recv.at[q],
            device_id={"pipe": p + 1}, device_id_type=MESH)

    def chain_store(q):
        _, _, rows = place(q, CHUNK)
        return pltpu.make_async_copy(out_v.at[rows, :], cot_hbm.at[rows, :], st_sem.at[q])

    def chain_step(q, carry):
        s, t, rows = place(q, CHUNK)

        @pl.when(jnp.logical_not(is_last))
        def _():
            chain_recv(q).wait_recv()

        g = a_v[rows, RES]
        hg = hs_v[rows, :] + dot(g, wt_v[CONV:, :])
        pg1 = (hg * a1_v[rows, :]).astype(BF16)
        pg2 = (hg * a2_v[rows, :]).astype(BF16)
        a_v[rows, 0:C] = pg1
        a_v[rows, C:2 * C] = pg2
        prow = pl.ds(pl.multiple_of(s * STRIDE + t, 8), CHUNK)
        pf_v[prow, 0:C] = pg1.astype(F32)
        pf_v[prow, C:2 * C] = pg2.astype(F32)
        a_v[rows, 1024:2048] = advanced(s, t, d)
        a_v[rows, 2048:3072] = advanced(s, t, 2 * d)
        out = g.astype(F32) + dot(a_v[rows, 0:CONV], wt_v[0:CONV, :])
        out_v[rows, :] = out.astype(BF16)

        @pl.when(jnp.logical_not(is_first))
        def _():
            chain_send(q).start()

        chain_store(q).start()

        more = jnp.logical_and(lax.rem(q, RATIO) == RATIO - 1, q < CHUNKS - 1)

        @pl.when(jnp.logical_and(is_last, more))
        def _():
            forward(jnp.minimum((q + 1) // RATIO, AHEADS - 1))

        return carry

    def grad_step(lhs_v, s, add, n, carry):
        lanes = pl.ds(pl.multiple_of(n * C, C), C)
        rows = slice(s * LEN, (s + 1) * LEN)
        term = dot(lhs_v[:, rows], a_v[rows, lanes])
        g_v[:, lanes] = g_v[:, lanes] + term if add else term
        return carry

    def grads(s, add):
        lax.fori_loop(0, 6, functools.partial(grad_step, xt_v, s, add), 0)
        lax.fori_loop(6, 8, functools.partial(grad_step, ht_v, s, add), 0)

    early = p < 2
    lax.fori_loop(0, PER_SEQ, chain_step, 0)

    @pl.when(early)
    def _():
        grads(0, False)

    lax.fori_loop(PER_SEQ, CHUNKS, chain_step, 0)

    @pl.when(jnp.logical_not(early))
    def _():
        grads(0, False)

    grads(1, True)

    rs_tasks, rs_order, _ = scatter
    starts = (0, RS_SPLIT)
    recv_bufs, send_bufs = (ra_v, rb_v), (sa_v, sb_v)

    def rs_copy(key):
        task = rs_tasks[key]
        group, slot, sem = slots[key]
        lo = task["piece"][0] - starts[group]
        lanes = slice(lo, lo + task["piece"][1])
        source = send_bufs[group].at[slot, :, lanes]
        target = recv_bufs[group].at[slot, :, lanes]
        return pltpu.make_async_remote_copy(
            source, target, rs_send.at[sem], rs_recv.at[sem],
            device_id=peer(task["axis"], task["way"]), device_id_type=MESH)

    def rs_take(key):
        task = rs_tasks[key]
        group, slot, sem = slots[key]
        lo = task["piece"][0] - starts[group]
        view = recv_bufs[group].at[slot, :, lo:lo + task["piece"][1]]
        pltpu.make_async_remote_copy(
            view, view, rs_send.at[sem], rs_recv.at[sem],
            device_id=peer(task["axis"], -task["way"]), device_id_type=MESH).wait_recv()
        return group, slot, task["piece"]

    for key in rs_order:
        task = rs_tasks[key]
        rows = rows_at({"z": task["block"]["z"], "y": task["block"]["y"]})
        first, count = task["piece"]
        got = [rs_take(need) for need in task["recvs"]]
        if task["axis"] is None:
            total = g_v[rows, first:first + count]
            for group, slot, piece in got:
                total = total + recv_bufs[group][slot, :, 0:count].astype(F32)
            g_v[rows, first:first + count] = total
            continue
        group, slot, _ = slots[key]
        base = starts[group]
        spans = [(first, count, None)]
        if got:
            _, have, (p0, pn) = got[0]
            spans = [(p0, pn, have)]
            if p0 > first:
                spans.append((first, p0 - first, None))
            if p0 + pn < first + count:
                spans.append((p0 + pn, first + count - p0 - pn, None))
        for lo, n, have in spans:
            value = g_v[rows, lo:lo + n]
            if have is not None:
                value = value + recv_bufs[group][have, :, lo - base:lo - base + n].astype(F32)
            send_bufs[group][slot, :, lo - base:lo - base + n] = value.astype(BF16)
        rs_copy(key).start()

    own_rows = rows_at({"z": 0, "y": 0})
    grad_stores = [
        pltpu.make_async_copy(
            g_v.at[own_rows, k * 1024:(k + 1) * 1024], conv_hbm.at[k] if k < 3 else mix_hbm, ld_sem.at[k])
        for k in range(4)
    ]
    for store in grad_stores:
        store.start()

    for ident in range(len(ag_sends)):
        ag_send_copy(ident).wait_send()
    for key in rs_order:
        if rs_tasks[key]["axis"] is not None:
            rs_copy(key).wait_send()
    for q in range(CHUNKS):
        chain_store(q).wait()

        @pl.when(jnp.logical_not(is_first))
        def _():
            chain_send(q).wait_send()

    for store in grad_stores:
        store.wait()


def local(x_ckpt, top_cot, skip_cot, w_conv, w_mix):
    x = x_ckpt.reshape(ROWS, C)
    top = top_cot.reshape(ROWS, C)
    skip = skip_cot.reshape(ROWS, C)
    taps = w_conv.reshape(SHARD, 3, 2 * C).transpose(1, 0, 2)
    mix = w_mix.reshape(SHARD, 2 * C)
    gather = gather2(AG_SPLIT, WIDTH, SHARD, 53e3, 2.4, 0.0, (1, 1))
    scatter = scatter2(RS_SPLIT, WIDTH, SHARD, 53e3, 2.4, 2e-6, 0.0, (1, 1))
    slots, counts, sems = {}, [0, 0], 0
    for key, task in scatter[0].items():
        if task["axis"] is not None:
            slots[key] = (key[0], counts[key[0]], sems)
            counts[key[0]] += 1
            sems += 1
    sends = len(gather[0])
    anywhere = pl.BlockSpec(memory_space=pl.ANY)
    dma = pltpu.SemaphoreType.DMA
    cot, conv_grad, mix_grad = pl.pallas_call(
        functools.partial(kernel, gather, scatter, slots),
        out_shape=(
            jax.ShapeDtypeStruct((ROWS, C), BF16),
            jax.ShapeDtypeStruct((3, SHARD, 2 * C), F32),
            jax.ShapeDtypeStruct((SHARD, 2 * C), F32),
        ),
        in_specs=[anywhere] * 5,
        out_specs=(anywhere,) * 3,
        scratch_shapes=[
            pltpu.VMEM((C, WIDTH), BF16),
            pltpu.VMEM((CONV + C, C), BF16),
            pltpu.VMEM((ROWS, C), BF16),
            pltpu.VMEM((2 * STRIDE, C), F32),
            pltpu.VMEM((C, ROWS), BF16),
            pltpu.VMEM((C, ROWS), BF16),
            pltpu.VMEM((ROWS, C), F32),
            pltpu.VMEM((ROWS, C), F32),
            pltpu.VMEM((ROWS, C), F32),
            pltpu.VMEM((2 * STRIDE, 2 * C), F32),
            pltpu.VMEM((ROWS, WIDTH), BF16),
            pltpu.VMEM((ROWS, C), BF16),
            pltpu.VMEM((C, WIDTH), F32),
            pltpu.VMEM((counts[0], SHARD, RS_SPLIT), BF16),
            pltpu.VMEM((counts[1], SHARD, WIDTH - RS_SPLIT), BF16),
            pltpu.VMEM((counts[0], SHARD, RS_SPLIT), BF16),
            pltpu.VMEM((counts[1], SHARD, WIDTH - RS_SPLIT), BF16),
            dma((sends,)), dma((sends,)), dma((sems,)), dma((sems,)),
            dma((CHUNKS,)), dma((CHUNKS,)), dma((7,)), dma((CHUNKS,)),
        ],
        compiler_params=pltpu.CompilerParams(
            collective_id=0, has_side_effects=True, vmem_limit_bytes=67043328),
    )(x, top, skip, taps, mix)
    return (
        cot.reshape(x_ckpt.shape),
        conv_grad.transpose(1, 0, 2).reshape(w_conv.shape),
        mix_grad.reshape(w_mix.shape),
    )


def solution(mesh):
    placed = (
        P("pipe", None, "dp", None, None),
        P(None, "dp", None, None),
        P(None, "dp", None, None),
        P("pipe", "dp", None, None),
        P("pipe", "dp", None),
    )
    return jax.shard_map(
        local,
        mesh=mesh,
        in_specs=placed,
        out_specs=(
            P("pipe", None, "dp", None, None),
            P("pipe", "dp", None, None),
            P("pipe", "dp", None),
        ),
        check_vma=False,
    )
```

```python
import functools
import heapq

import jax
import jax.numpy as jnp
from jax import lax
from jax.experimental import pallas as pl
from jax.experimental.pallas import tpu as pltpu
from jax.sharding import PartitionSpec as P

NZ, NY = 8, 4
UNIT = 128


def halves(piece):
    start, count = piece
    first = (count // UNIT + 1) // 2 * UNIT
    return (start, first), (start + first, count - first)


def wrap(offset, count):
    return (offset + count // 2 - 1) % count - (count // 2 - 1)


def gather_plan(split, width, rows, rate, lag):
    sizes = {"z": NZ, "y": NY}
    free, events, sends, order = {}, [], [], []
    seq = 0

    def send(now, group, axis, way, offset, piece):
        nonlocal seq
        if piece[1] == 0:
            return
        key = (axis, way)
        begin = max(now, free.get(key, 0.0))
        free[key] = begin + rows * piece[1] * 2 / rate
        ident = len(sends)
        shift = dict(offset)
        shift[axis] = wrap(shift[axis] - way, sizes[axis])
        sends.append((axis, way, dict(offset), shift, piece))
        order.append(("send", ident))
        heapq.heappush(events, (free[key] + lag, ident, group))
        seq += 1

    axes = (("z", "y"), ("y", "z"))
    pieces = ((0, split), (split, width - split))
    here = {"z": 0, "y": 0}
    for group in (0, 1):
        for way in (1, -1):
            send(0.0, group, axes[group][0], way, here, pieces[group])
    for group in (0, 1):
        for way in (1, -1):
            send(0.0, group, axes[group][1], way, here, pieces[group])
    last = 0.0
    while events:
        now, ident, group = heapq.heappop(events)
        last = now
        axis, way, _, offset, piece = sends[ident]
        order.append(("wait", ident))
        reach = sizes[axis] // 2
        done = abs(offset[axis]) if offset[axis] != reach else reach
        if done < reach - 1:
            send(now, group, axis, way, offset, piece)
        elif done == reach - 1:
            send(now, group, axis, way, offset, halves(piece)[0 if way > 0 else 1])
        if axis == axes[group][0]:
            for side in (1, -1):
                send(now, group, axes[group][1], side, offset, piece)
    return sends, order, last


def scatter_plan(split, width, rows, rate, lag, cost):
    sizes = {"z": NZ, "y": NY}
    axes = (("z", "y"), ("y", "z"))
    pieces = ((0, split), (split, width - split))
    tasks = {}
    for group in (0, 1):
        one, two = axes[group]
        h1, h2 = sizes[one] // 2, sizes[two] // 2
        part1 = halves(pieces[group])
        others = [h2] + [s * j for j in range(h2 - 1, 0, -1) for s in (1, -1)] + [0]
        for rank, o2 in enumerate(others):
            for way in (1, -1):
                for j in range(h1, 0, -1):
                    piece = pieces[group] if j < h1 else part1[0 if way > 0 else 1]
                    needs = [(group, 1, way, j + 1, o2)] if j < h1 else []
                    tasks[(group, 1, way, j, o2)] = dict(
                        axis=one, way=way, block={one: way * j, two: o2}, piece=piece,
                        recvs=needs, locals=[], rank=(rank, -j))
            tasks[(group, 1, 0, 0, o2)] = dict(
                axis=None, way=0, block={one: 0, two: o2}, piece=pieces[group],
                recvs=[(group, 1, 1, 1, o2), (group, 1, -1, 1, o2)], locals=[], rank=(rank, 0))
        for way in (1, -1):
            for j in range(h2, 0, -1):
                piece = pieces[group] if j < h2 else part1[0 if way > 0 else 1]
                needs = [(group, 2, way, j + 1, 0)] if j < h2 else []
                at = way * j if j < h2 else h2
                tasks[(group, 2, way, j, 0)] = dict(
                    axis=two, way=way, block={one: 0, two: at}, piece=piece,
                    recvs=needs, locals=[(group, 1, 0, 0, at)], rank=(-1, -j))
        tasks[(group, 2, 0, 0, 0)] = dict(
            axis=None, way=0, block={one: 0, two: 0}, piece=pieces[group],
            recvs=[(group, 2, 1, 1, 0), (group, 2, -1, 1, 0)], locals=[(group, 1, 0, 0, 0)], rank=(-1, 0))
    arrive, finished, free, order, clock = {}, {}, {}, [], 0.0
    left = dict(tasks)
    while left:
        best = None
        for key, task in left.items():
            if any(n not in arrive for n in task["recvs"]) or any(n not in finished for n in task["locals"]):
                continue
            ready = max([clock] + [arrive[n] for n in task["recvs"]] + [finished[n] for n in task["locals"]])
            link = free.get((task["axis"], task["way"]), 0.0) if task["axis"] else 0.0
            score = (ready, task["rank"], link, key)
            if best is None or score < best[0]:
                best = (score, key, ready)
        _, key, ready = best
        task = left.pop(key)
        clock = ready + cost * rows * task["piece"][1]
        finished[key] = clock
        if task["axis"]:
            lane = (task["axis"], task["way"])
            begin = max(clock, free.get(lane, 0.0))
            free[lane] = begin + rows * task["piece"][1] * 2 / rate
            arrive[key] = free[lane] + lag
        order.append(key)
    return tasks, order, clock


def gather2(split, width, rows, rate, lag, ahead, wts):
    sizes = {"z": NZ, "y": NY}
    axes = (("z", "y"), ("y", "z"))
    pieces = ((0, split), (split, width - split))
    links = {(a, w): [] for a in "zy" for w in (1, -1)}
    free = {k: 0.0 for k in links}
    sends, order, events = [], [], []
    tick = 0
    def offer(now, group, axis, way, offset, piece):
        nonlocal tick
        if piece[1] == 0: return
        reach = sizes[axis] // 2
        gone = abs(offset[axis])
        left = reach - gone
        two = axes[group][1]
        follow = sizes[two] // 2 if axis == axes[group][0] else 0
        score = -(left * wts[0] + follow * wts[1])
        tick += 1
        heapq.heappush(links[(axis, way)], (score, tick, now, group, dict(offset), piece))
    here = {"z": 0, "y": 0}
    for group in (0, 1):
        for axis in axes[group]:
            for way in (1, -1):
                offer(0.0, group, axis, way, here, pieces[group])
    now = 0.0
    last = 0.0
    while True:
        for key, queue in links.items():
            while queue and free[key] <= now + ahead + 1e-6:
                score, _, _, group, offset, piece = heapq.heappop(queue)
                axis, way = key
                begin = max(now, free[key])
                free[key] = begin + rows * piece[1] * 2 / rate
                ident = len(sends)
                shift = dict(offset); shift[axis] = wrap(shift[axis] - way, sizes[axis])
                sends.append((axis, way, dict(offset), shift, piece))
                order.append(("send", ident))
                heapq.heappush(events, (free[key] + lag, 0, ident, group))
        nxt = [free[k] - ahead for k, q in links.items() if q]
        t = min(nxt) if nxt else float("inf")
        if events and events[0][0] <= t:
            now, _, ident, group = heapq.heappop(events)
            last = max(last, now)
            axis, way, _, offset, piece = sends[ident]
            order.append(("wait", ident))
            reach = sizes[axis] // 2
            done = abs(offset[axis])
            if done < reach - 1: offer(now, group, axis, way, offset, piece)
            elif done == reach - 1: offer(now, group, axis, way, offset, halves(piece)[0 if way > 0 else 1])
            if axis == axes[group][0]:
                for side in (1, -1): offer(now, group, axes[group][1], side, offset, piece)
        elif nxt:
            now = max(now, t)
        else:
            break
    return sends, order, last


def scatter2(split, width, rows, rate, lag, cost, ahead, wts):
    tasks = scatter_plan(split, width, rows, rate, lag, cost)[0]
    needs, users = {}, {}
    for key, task in tasks.items():
        deps = [("r", n) for n in task["recvs"]] + [("l", n) for n in task["locals"]]
        needs[key] = len(deps)
        for kind, n in deps:
            users.setdefault((kind, n), []).append(key)
    links = {(a, w): [] for a in "zy" for w in (1, -1)}
    free = {k: 0.0 for k in links}
    order, events = [], []
    def remaining(key):
        group, stage, way, j, o2 = key
        return wts[0] * j + wts[1] * abs(o2) * (stage == 1)
    def ready(key, now):
        task = tasks[key]
        if task["axis"] is None:
            order.append(key)
            heapq.heappush(events, (now + cost * rows * task["piece"][1], "l", key))
        else:
            heapq.heappush(links[(task["axis"], task["way"])], (-remaining(key), len(order), key))
    now = 0.0
    for key in tasks:
        if needs[key] == 0: ready(key, 0.0)
    last = 0.0
    while True:
        for link, queue in links.items():
            while queue and free[link] <= now + ahead + 1e-6:
                key = heapq.heappop(queue)[2]
                begin = max(now, free[link])
                free[link] = begin + rows * tasks[key]["piece"][1] * 2 / rate
                order.append(key)
                heapq.heappush(events, (free[link] + lag, "r", key))
        nxt = [free[k] - ahead for k, q in links.items() if q]
        t = min(nxt) if nxt else float("inf")
        if events and events[0][0] <= t:
            now, kind, key = heapq.heappop(events)
            last = max(last, now)
            for user in users.get((kind, key), []):
                needs[user] -= 1
                if needs[user] == 0: ready(user, now)
        elif nxt:
            now = max(now, t)
        else:
            break
    assert len(order) == len(tasks)
    return tasks, order, last


F32, BF16 = jnp.float32, jnp.bfloat16
MESH = pl.DeviceIdType.MESH
SECTIONS = 8
C = 512
LEN = 512
ROWS = 1024
SHARD = 16
WIDTH = 4096
CONV = 3072
RES = slice(3072, 3584)
SKIP = slice(3584, 4096)
CHUNK = 128
AHEAD = 256
CHUNKS = ROWS // CHUNK
AHEADS = ROWS // AHEAD
RATIO = AHEAD // CHUNK
PER_SEQ = LEN // CHUNK
PAD = 264
STRIDE = LEN + PAD
RATE, LAG = 46.5e3, 1.8
AG_SPLIT, RS_SPLIT = 2560, 1536
NT = (((1,), (1,)), ((), ()))


def dot(a, b):
    return jnp.dot(a, b, preferred_element_type=F32)


def dot_nt(a, b):
    return lax.dot_general(a, b, NT, preferred_element_type=F32)


def kernel(gather, scatter, slots, x_hbm, top_hbm, skip_hbm, wc_hbm, wm_hbm, cot_hbm, conv_hbm, mix_hbm,
           w_v, wt_v, x_v, xf_v, xt_v, ht_v, a1_v, a2_v, hs_v, pf_v, a_v, out_v, g_v,
           ra_v, rb_v, sa_v, sb_v,
           ag_send, ag_recv, rs_send, rs_recv, ch_send, ch_recv, ld_sem, st_sem):
    p = lax.axis_index("pipe")
    dp = lax.axis_index("dp")
    z, y = dp // NY, lax.rem(dp, NY)

    def dp_at(dz, dy):
        return lax.rem(z + (dz + NZ), NZ) * NY + lax.rem(y + (dy + NY), NY)

    def rows_at(offset):
        return pl.ds(pl.multiple_of(dp_at(offset["z"], offset["y"]) * SHARD, SHARD), SHARD)

    def peer(axis, way):
        return {"dp": dp_at(way, 0) if axis == "z" else dp_at(0, way)}

    is_last, is_first = p == SECTIONS - 1, p == 0

    x_load = pltpu.make_async_copy(x_hbm, x_v, ld_sem.at[0])
    skip_load = pltpu.make_async_copy(skip_hbm, a_v.at[:, SKIP], ld_sem.at[1])
    top_load = pltpu.make_async_copy(top_hbm, a_v.at[:, RES], ld_sem.at[2])
    own = rows_at({"z": 0, "y": 0})
    own_loads = [
        pltpu.make_async_copy(
            wc_hbm.at[k] if k < 3 else wm_hbm, w_v.at[own, k * 1024:(k + 1) * 1024], ld_sem.at[3 + k])
        for k in range(4)
    ]
    for load in own_loads:
        load.start()
    x_load.start()
    skip_load.start()

    @pl.when(is_last)
    def _():
        top_load.start()

    barrier = pltpu.get_barrier_semaphore()
    for axis in ("z", "y"):
        for way in (1, -1):
            pl.semaphore_signal(barrier, inc=1, device_id=peer(axis, way), device_id_type=MESH)

    for way in (1, SECTIONS - 1):
        neighbour = {"pipe": lax.rem(p + way, SECTIONS)}
        pl.semaphore_signal(barrier, inc=1, device_id=neighbour, device_id_type=MESH)
    for load in own_loads:
        load.wait()
    pl.semaphore_wait(barrier, 6)

    ag_sends, ag_order, _ = gather

    def ag_send_copy(ident):
        axis, way, offset, _, piece = ag_sends[ident]
        lanes = slice(piece[0], piece[0] + piece[1])
        here = w_v.at[rows_at(offset), lanes]
        return pltpu.make_async_remote_copy(
            here, here, ag_send.at[ident], ag_recv.at[ident],
            device_id=peer(axis, way), device_id_type=MESH)

    def ag_recv_copy(ident):
        axis, way, _, landed, piece = ag_sends[ident]
        lanes = slice(piece[0], piece[0] + piece[1])
        there = w_v.at[rows_at(landed), lanes]
        return pltpu.make_async_remote_copy(
            there, there, ag_send.at[ident], ag_recv.at[ident],
            device_id=peer(axis, -way), device_id_type=MESH)

    started = False
    for what, ident in ag_order:
        if what == "send":
            ag_send_copy(ident).start()
            continue
        if not started:
            started = True
            x_load.wait()
            for s in range(2):
                xf_v[s * STRIDE:s * STRIDE + PAD, :] = jnp.zeros((PAD, C), F32)
                xf_v[s * STRIDE + PAD:(s + 1) * STRIDE, :] = x_v[s * LEN:(s + 1) * LEN, :].astype(F32)
                pf_v[s * STRIDE + LEN:(s + 1) * STRIDE, :] = jnp.zeros((PAD, 2 * C), F32)
        ag_recv_copy(ident).wait_recv()
    skip_load.wait()

    d = (1 + lax.rem(p, 2)) * (1 + 3 * lax.rem(p // 2, 2)) * (1 + 15 * (p // 4))

    def shifted(ref, base, down, size):
        window = ref[pl.ds(pl.multiple_of(base, 8), size + 8), :]
        width = window.shape[1]
        turned = pltpu.roll(window.reshape(size // 8 + 1, 8, width), down, 1)
        inner = lax.broadcasted_iota(jnp.int32, (size // 8, 8, width), 1) >= down
        return jnp.where(inner, turned[1:], turned[:-1]).reshape(size, width).astype(BF16)

    def delayed(s, t, shift):
        down = lax.rem(shift, 8)
        return shifted(xf_v, s * STRIDE + PAD + t - (shift - down) - 8, down, AHEAD)

    def advanced(s, t, shift):
        down = lax.rem(8 - lax.rem(shift, 8), 8)
        return shifted(pf_v, s * STRIDE + t + (shift + down) - 8, down, CHUNK)

    def place(q, size):
        per = LEN // size
        s = q // per
        t = (per - 1 - lax.rem(q, per)) * size
        row = pl.multiple_of(s * LEN + t, size)
        return s, t, pl.ds(row, size)

    def forward(q):
        s, t, rows = place(q, AHEAD)
        x0 = x_v[rows, :]
        pre = dot(x0, w_v[:, 0:1024])
        pre = pre + dot(delayed(s, t, d), w_v[:, 1024:2048])
        pre = pre + dot(delayed(s, t, 2 * d), w_v[:, 2048:3072])
        filt = jnp.tanh(pre[:, :C])
        gate = jax.nn.sigmoid(pre[:, C:])
        a1_v[rows, :] = gate * (1.0 - filt * filt)
        hid = filt * gate
        a2_v[rows, :] = hid * (1.0 - gate)
        ht_v[:, rows] = hid.astype(BF16).T
        xt_v[:, rows] = x0.T
        hs_v[rows, :] = dot_nt(a_v[rows, SKIP], w_v[:, SKIP])

    def forward_step(q, carry):
        forward(q)
        return carry

    lax.fori_loop(0, jnp.where(is_last, 1, AHEADS), forward_step, 0)

    def turn_step(n, carry):
        lanes = pl.ds(pl.multiple_of(n * C, C), C)
        wt_v[lanes, :] = w_v[:, lanes].T
        return carry

    lax.fori_loop(0, (CONV + C) // C, turn_step, 0)

    @pl.when(is_last)
    def _():
        top_load.wait()

    def chain_send(q):
        _, _, rows = place(q, CHUNK)
        return pltpu.make_async_remote_copy(
            out_v.at[rows, :], a_v.at[rows, RES], ch_send.at[q], ch_recv.at[q],
            device_id={"pipe": p - 1}, device_id_type=MESH)

    def chain_recv(q):
        _, _, rows = place(q, CHUNK)
        return pltpu.make_async_remote_copy(
            a_v.at[rows, RES], a_v.at[rows, RES], ch_send.at[q], ch_recv.at[q],
            device_id={"pipe": p + 1}, device_id_type=MESH)

    def chain_store(q):
        _, _, rows = place(q, CHUNK)
        return pltpu.make_async_copy(out_v.at[rows, :], cot_hbm.at[rows, :], st_sem.at[q])

    def chain_step(q, carry):
        s, t, rows = place(q, CHUNK)

        @pl.when(jnp.logical_not(is_last))
        def _():
            chain_recv(q).wait_recv()

        g = a_v[rows, RES]
        hg = hs_v[rows, :] + dot(g, wt_v[CONV:, :])
        pg1 = (hg * a1_v[rows, :]).astype(BF16)
        pg2 = (hg * a2_v[rows, :]).astype(BF16)
        a_v[rows, 0:C] = pg1
        a_v[rows, C:2 * C] = pg2
        prow = pl.ds(pl.multiple_of(s * STRIDE + t, 8), CHUNK)
        pf_v[prow, 0:C] = pg1.astype(F32)
        pf_v[prow, C:2 * C] = pg2.astype(F32)
        a_v[rows, 1024:2048] = advanced(s, t, d)
        a_v[rows, 2048:3072] = advanced(s, t, 2 * d)
        out = g.astype(F32) + dot(a_v[rows, 0:CONV], wt_v[0:CONV, :])
        out_v[rows, :] = out.astype(BF16)

        @pl.when(jnp.logical_not(is_first))
        def _():
            chain_send(q).start()

        chain_store(q).start()

        more = jnp.logical_and(lax.rem(q, RATIO) == RATIO - 1, q < CHUNKS - 1)

        @pl.when(jnp.logical_and(is_last, more))
        def _():
            forward(jnp.minimum((q + 1) // RATIO, AHEADS - 1))

        return carry

    def grad_step(lhs_v, s, add, n, carry):
        lanes = pl.ds(pl.multiple_of(n * C, C), C)
        rows = slice(s * LEN, (s + 1) * LEN)
        term = dot(lhs_v[:, rows], a_v[rows, lanes])
        g_v[:, lanes] = g_v[:, lanes] + term if add else term
        return carry

    def grads(s, add):
        lax.fori_loop(0, 6, functools.partial(grad_step, xt_v, s, add), 0)
        lax.fori_loop(6, 8, functools.partial(grad_step, ht_v, s, add), 0)

    early = p < 2
    lax.fori_loop(0, PER_SEQ, chain_step, 0)

    @pl.when(early)
    def _():
        grads(0, False)

    lax.fori_loop(PER_SEQ, CHUNKS, chain_step, 0)

    @pl.when(jnp.logical_not(early))
    def _():
        grads(0, False)

    grads(1, True)

    rs_tasks, rs_order, _ = scatter
    starts = (0, RS_SPLIT)
    recv_bufs, send_bufs = (ra_v, rb_v), (sa_v, sb_v)

    def rs_copy(key):
        task = rs_tasks[key]
        group, slot, sem = slots[key]
        lo = task["piece"][0] - starts[group]
        lanes = slice(lo, lo + task["piece"][1])
        source = send_bufs[group].at[slot, :, lanes]
        target = recv_bufs[group].at[slot, :, lanes]
        return pltpu.make_async_remote_copy(
            source, target, rs_send.at[sem], rs_recv.at[sem],
            device_id=peer(task["axis"], task["way"]), device_id_type=MESH)

    def rs_take(key):
        task = rs_tasks[key]
        group, slot, sem = slots[key]
        lo = task["piece"][0] - starts[group]
        view = recv_bufs[group].at[slot, :, lo:lo + task["piece"][1]]
        pltpu.make_async_remote_copy(
            view, view, rs_send.at[sem], rs_recv.at[sem],
            device_id=peer(task["axis"], -task["way"]), device_id_type=MESH).wait_recv()
        return group, slot, task["piece"]

    for key in rs_order:
        task = rs_tasks[key]
        rows = rows_at({"z": task["block"]["z"], "y": task["block"]["y"]})
        first, count = task["piece"]
        got = [rs_take(need) for need in task["recvs"]]
        if task["axis"] is None:
            total = g_v[rows, first:first + count]
            for group, slot, piece in got:
                total = total + recv_bufs[group][slot, :, 0:count].astype(F32)
            g_v[rows, first:first + count] = total
            continue
        group, slot, _ = slots[key]
        base = starts[group]
        spans = [(first, count, None)]
        if got:
            _, have, (p0, pn) = got[0]
            spans = [(p0, pn, have)]
            if p0 > first:
                spans.append((first, p0 - first, None))
            if p0 + pn < first + count:
                spans.append((p0 + pn, first + count - p0 - pn, None))
        for lo, n, have in spans:
            value = g_v[rows, lo:lo + n]
            if have is not None:
                value = value + recv_bufs[group][have, :, lo - base:lo - base + n].astype(F32)
            send_bufs[group][slot, :, lo - base:lo - base + n] = value.astype(BF16)
        rs_copy(key).start()

    own_rows = rows_at({"z": 0, "y": 0})
    grad_stores = [
        pltpu.make_async_copy(
            g_v.at[own_rows, k * 1024:(k + 1) * 1024], conv_hbm.at[k] if k < 3 else mix_hbm, ld_sem.at[k])
        for k in range(4)
    ]
    for store in grad_stores:
        store.start()

    for ident in range(len(ag_sends)):
        ag_send_copy(ident).wait_send()
    for key in rs_order:
        if rs_tasks[key]["axis"] is not None:
            rs_copy(key).wait_send()
    for q in range(CHUNKS):
        chain_store(q).wait()

        @pl.when(jnp.logical_not(is_first))
        def _():
            chain_send(q).wait_send()

    for store in grad_stores:
        store.wait()


def hand_out(cot_in, conv_in, mix_in, cot_out, conv_out, mix_out, cot_v, conv_v, mix_v, load_sem, store_sem):
    quarter = ROWS // 4
    parts = [
        tuple(ref.at[pl.ds(k * quarter, quarter)] for ref in (cot_in, cot_v, cot_out)) for k in range(4)
    ] + [(conv_in, conv_v, conv_out), (mix_in, mix_v, mix_out)]
    moves = []
    for k, part in enumerate(parts):
        source, middle, target = part
        load = pltpu.make_async_copy(source, middle, load_sem.at[k])
        load.start()
        moves.append((load, pltpu.make_async_copy(middle, target, store_sem.at[k])))
    for load, store in moves:
        load.wait()
        store.start()
    for _, store in moves:
        store.wait()


def local(x_ckpt, top_cot, skip_cot, w_conv, w_mix):
    x = x_ckpt.reshape(ROWS, C)
    top = top_cot.reshape(ROWS, C)
    skip = skip_cot.reshape(ROWS, C)
    taps = w_conv.reshape(SHARD, 3, 2 * C).transpose(1, 0, 2)
    mix = w_mix.reshape(SHARD, 2 * C)
    gather = gather2(AG_SPLIT, WIDTH, SHARD, 53e3, 2.4, 0.0, (1, 1))
    scatter = scatter2(RS_SPLIT, WIDTH, SHARD, 53e3, 2.4, 2e-6, 0.0, (1, 1))
    slots, counts, sems = {}, [0, 0], 0
    for key, task in scatter[0].items():
        if task["axis"] is not None:
            slots[key] = (key[0], counts[key[0]], sems)
            counts[key[0]] += 1
            sems += 1
    sends = len(gather[0])
    anywhere = pl.BlockSpec(memory_space=pl.ANY)
    dma = pltpu.SemaphoreType.DMA
    cot, conv_grad, mix_grad = pl.pallas_call(
        functools.partial(kernel, gather, scatter, slots),
        out_shape=(
            jax.ShapeDtypeStruct((ROWS, C), BF16),
            jax.ShapeDtypeStruct((3, SHARD, 2 * C), F32),
            jax.ShapeDtypeStruct((SHARD, 2 * C), F32),
        ),
        in_specs=[anywhere] * 5,
        out_specs=(anywhere,) * 3,
        scratch_shapes=[
            pltpu.VMEM((C, WIDTH), BF16),
            pltpu.VMEM((CONV + C, C), BF16),
            pltpu.VMEM((ROWS, C), BF16),
            pltpu.VMEM((2 * STRIDE, C), F32),
            pltpu.VMEM((C, ROWS), BF16),
            pltpu.VMEM((C, ROWS), BF16),
            pltpu.VMEM((ROWS, C), F32),
            pltpu.VMEM((ROWS, C), F32),
            pltpu.VMEM((ROWS, C), F32),
            pltpu.VMEM((2 * STRIDE, 2 * C), F32),
            pltpu.VMEM((ROWS, WIDTH), BF16),
            pltpu.VMEM((ROWS, C), BF16),
            pltpu.VMEM((C, WIDTH), F32),
            pltpu.VMEM((counts[0], SHARD, RS_SPLIT), BF16),
            pltpu.VMEM((counts[1], SHARD, WIDTH - RS_SPLIT), BF16),
            pltpu.VMEM((counts[0], SHARD, RS_SPLIT), BF16),
            pltpu.VMEM((counts[1], SHARD, WIDTH - RS_SPLIT), BF16),
            dma((sends,)), dma((sends,)), dma((sems,)), dma((sems,)),
            dma((CHUNKS,)), dma((CHUNKS,)), dma((7,)), dma((CHUNKS,)),
        ],
        compiler_params=pltpu.CompilerParams(
            collective_id=0, has_side_effects=True, vmem_limit_bytes=67043328),
    )(x, top, skip, taps, mix)
    results = (cot, conv_grad, mix_grad)
    cot, conv_grad, mix_grad = pl.pallas_call(
        hand_out,
        out_shape=tuple(jax.ShapeDtypeStruct(r.shape, r.dtype) for r in results),
        in_specs=[anywhere] * 3,
        out_specs=(anywhere,) * 3,
        scratch_shapes=[pltpu.VMEM(r.shape, r.dtype) for r in results] + [dma((6,)), dma((6,))],
        compiler_params=pltpu.CompilerParams(vmem_limit_bytes=67043328),
    )(*results)
    return (
        cot.reshape(x_ckpt.shape),
        conv_grad.transpose(1, 0, 2).reshape(w_conv.shape),
        mix_grad.reshape(w_mix.shape),
    )


def solution(mesh):
    placed = (
        P("pipe", None, "dp", None, None),
        P(None, "dp", None, None),
        P(None, "dp", None, None),
        P("pipe", "dp", None, None),
        P("pipe", "dp", None),
    )
    return jax.shard_map(
        local,
        mesh=mesh,
        in_specs=placed,
        out_specs=(
            P("pipe", None, "dp", None, None),
            P("pipe", "dp", None, None),
            P("pipe", "dp", None),
        ),
        check_vma=False,
    )
```
